32 devices in a mesh: tower: 2 (over core), blk: 8 (over z, x), seq: 2 (over y).
Axes of the slice: x: 2, y: 2, z: 4, core: 2. Of those that a mesh axis runs over, the one named last changes fastest.
Arguments:
- queries: bfloat16 [2, 2048, 1024], P('tower', ('blk', 'seq')), may hold values from -6 to 6
- key_rows: bfloat16 [2, 2048, 1024], P('tower', ('blk', 'seq')), may hold values from -6 to 6
- value_rows: bfloat16 [2, 2048, 1024], P('tower', ('blk', 'seq')), may hold values from -6 to 6
- cross_queries: bfloat16 [2, 2048, 1024], P('tower', ('blk', 'seq')), may hold values from -6 to 6
- cross_keys: bfloat16 [2, 2048, 1024], P('tower', ('blk', 'seq')), may hold values from -6 to 6
- cross_values: bfloat16 [2, 2048, 1024], P('tower', ('blk', 'seq')), may hold values from -6 to 6
- grad_out: bfloat16 [2, 2048, 1024], P('tower', ('blk', 'seq')), may hold values from -6 to 6
- offsets: int32 [2, 8], replicated, may hold values from -127 to 127, as said below
- key_valid: int32 [2, 2048], P(None, ('blk', 'seq')), may hold values from 0 to 1, as said below
Outputs:
- attended: bfloat16 [2, 2048, 1024], P('tower', ('blk', 'seq'))
- grad_queries: bfloat16 [2, 2048, 1024], P('tower', ('blk', 'seq'))
- grad_keys: bfloat16 [2, 2048, 1024], P('tower', ('blk', 'seq'))
- grad_values: bfloat16 [2, 2048, 1024], P('tower', ('blk', 'seq'))
- grad_cross_queries: bfloat16 [2, 2048, 1024], P('tower', ('blk', 'seq'))
- grad_cross_keys: bfloat16 [2, 2048, 1024], P('tower', ('blk', 'seq'))
- grad_cross_values: bfloat16 [2, 2048, 1024], P('tower', ('blk', 'seq'))
The draws below stay inside these ranges and needn't reach their ends.
Inputs may be any that keep to these rules, and one draw needn't show every extreme that they name: Both ends of the range occur in every draw; for every block b, offsets[0, b] and offsets[1, b] have opposite signs, and every magnitude is at least 64. `key_valid`: positions k * 256 + 256 // 2 - 1 and k * 256 + 256 // 2 are always 1.
All inputs are finite; a program needn't handle non-finite values.
Results may differ from the reference program's by a relative error of at most 0.019.
Values may be sent and summed in bfloat16 or wider, within the bound.
A program may use at most 128 MiB of HBM per device.

```python
import jax
import jax.numpy as jnp
from jax import lax

HEADS = 16
HEAD = 64
D = 1024
LEN = 2048
BLOCK = 256
NBLOCKS = 8
HALF = 128
QT = 256


def background(key, salt):
    sub_key = jax.random.fold_in(key, salt)
    return jnp.clip(jax.random.normal(sub_key, (2, LEN, HEADS * HEAD), jnp.float32), -4.0, 4.0)


def draw_queries(key, part):
    field = background(key, 1)
    return field.astype(jnp.bfloat16)


def draw_key_rows(key, part):
    field = background(key, 2)
    return field.astype(jnp.bfloat16)


def draw_cross_queries(key, part):
    field = background(key, 3)
    return field.astype(jnp.bfloat16)


def draw_cross_keys(key, part):
    field = background(key, 4)
    return field.astype(jnp.bfloat16)


def draw_offsets(key, part):
    low_mag = max(HALF // 2, 1)
    magnitude = jax.random.randint(key, (2, NBLOCKS), low_mag, HALF)
    sign_first = 2 * jax.random.randint(jax.random.fold_in(key, 7), (NBLOCKS,), 0, 2) - 1
    spots = jax.random.randint(jax.random.fold_in(key, 5), (2,), 0, NBLOCKS)
    sign_first = sign_first.at[spots[0]].set(1).at[spots[1]].set(1)
    magnitude = magnitude.at[0, spots[0]].set(HALF - 1).at[1, spots[1]].set(HALF - 1)
    signs = jnp.stack((sign_first, -sign_first))
    return (signs * magnitude).astype(jnp.int32)


def draw_key_valid(key, part):
    coins = jax.random.randint(key, (2, LEN), 0, 8)
    phase = jnp.arange(LEN) % BLOCK
    keep = (phase == BLOCK // 2 - 1) | (phase == BLOCK // 2)
    return jnp.where(keep[None, :] | (coins > 0), 1, 0).astype(jnp.int32)


def level_of(key, extent, pieces, smallest, high):
    gain, own = 1.0, jax.random.fold_in(key, 6)
    for axis_at, blocks in pieces:
        draws = jnp.exp(jax.random.uniform(jax.random.fold_in(own, axis_at), (blocks,), jnp.float32, smallest / len(pieces), high / len(pieces)))
        gain = gain * jnp.repeat(draws, extent[axis_at] // blocks).reshape([-1 if axis == axis_at else 1 for axis in range(len(extent))])
    return gain


def gaussian(key, extent, width, bound, pieces=(), kind=jnp.bfloat16):
    factor_of = level_of(key, extent, pieces, -0.22, 0.18) if pieces else 1.0
    entries = jax.random.normal(key, extent, jnp.float32) * width * factor_of
    return jnp.minimum(jnp.maximum(entries, -bound), bound).astype(kind)


def setup_inputs(seed: int = 0) -> dict:
    splits = jax.random.split(jax.random.key(seed), 10)
    return {
        "queries": draw_queries(jax.random.fold_in(splits[9], 71), 0),
        "key_rows": draw_key_rows(jax.random.fold_in(splits[9], 71), 0),
        "value_rows": gaussian(splits[2], (2, LEN, D), 1.0, 6.0, ((0, 2), (1, 16))),
        "cross_queries": draw_cross_queries(jax.random.fold_in(splits[9], 71), 0),
        "cross_keys": draw_cross_keys(jax.random.fold_in(splits[9], 71), 0),
        "cross_values": gaussian(splits[5], (2, LEN, D), 1.0, 6.0, ((0, 2), (1, 16))),
        "grad_out": gaussian(splits[6], (2, LEN, D), 1.0, 6.0, ((0, 2), (1, 16))),
        "offsets": draw_offsets(jax.random.fold_in(splits[9], 71), 0),
        "key_valid": draw_key_valid(jax.random.fold_in(splits[9], 71), 0),
    }


def attend(query_tile, grad_tile, key_block, value_block, allowed, heads_here):
    score_scale = HEAD ** -0.5
    rows_count = query_tile.shape[0]
    keys_count = key_block.shape[0]
    q_heads = query_tile.reshape(rows_count, heads_here, HEAD).astype(jnp.float32)
    g_heads = grad_tile.reshape(rows_count, heads_here, HEAD).astype(jnp.float32)
    k_heads = key_block.reshape(keys_count, heads_here, HEAD).astype(jnp.float32)
    v_heads = value_block.reshape(keys_count, heads_here, HEAD).astype(jnp.float32)
    scores = jnp.einsum("qhe,khe->hqk", q_heads, k_heads) * score_scale
    scores = jnp.where(allowed[None], scores, -1e30)
    row_max = jnp.max(scores, axis=2)
    unnormed = jnp.exp(scores - row_max[:, :, None])
    row_sum = jnp.sum(unnormed, axis=2)
    weights = unnormed / row_sum[:, :, None]
    prob_bf = weights.astype(jnp.bfloat16).astype(jnp.float32)
    result = jnp.einsum("hqk,khe->qhe", prob_bf, v_heads).reshape(rows_count, -1)
    grad_probs = jnp.einsum("qhe,khe->hqk", g_heads, v_heads)
    row_dot = jnp.sum(weights * grad_probs, axis=2)
    grad_scores = (weights * (grad_probs - row_dot[:, :, None]) * score_scale).astype(jnp.bfloat16).astype(jnp.float32)
    grad_query = jnp.einsum("hqk,khe->qhe", grad_scores, k_heads).reshape(rows_count, -1)
    grad_key = jnp.einsum("hqk,qhe->khe", grad_scores, q_heads).reshape(keys_count, -1)
    grad_value = jnp.einsum("hqk,qhe->khe", prob_bf, g_heads).reshape(keys_count, -1)
    return result, grad_query, grad_key, grad_value


def reference(queries, key_rows, value_rows, cross_queries, cross_keys, cross_values, grad_out, offsets, key_valid):
    pad_rows = ((HALF, HALF), (0, 0))
    window_span = QT + 2 * HALF
    rows_local = jnp.arange(QT)
    keys_local = jnp.arange(window_span)
    near = jnp.abs(rows_local[:, None] + HALF - keys_local[None, :]) <= HALF
    tiles = jnp.arange(LEN // QT, dtype=jnp.int32)
    zeros_pad = jnp.zeros((LEN + 2 * HALF, HEADS * HEAD), jnp.float32)
    results = []
    cross_key_grads = [None, None]
    cross_value_grads = [None, None]
    for chain in range(2):
        other = 1 - chain
        key_pad = jnp.pad(key_rows[chain], pad_rows)
        value_pad = jnp.pad(value_rows[chain], pad_rows)
        valid_pad = jnp.pad(key_valid[chain], HALF)
        cross_key_pad = jnp.pad(cross_keys[other], pad_rows)
        cross_value_pad = jnp.pad(cross_values[other], pad_rows)
        other_valid = jnp.pad(key_valid[other], HALF)

        def self_step(carry, tile_index):
            grad_key_acc, grad_value_acc = carry
            tile_start = (tile_index * QT).astype(jnp.int32)
            query_tile = lax.dynamic_slice_in_dim(queries[chain], tile_start, QT, 0)
            grad_tile = lax.dynamic_slice_in_dim(grad_out[chain], tile_start, QT, 0)
            key_window = lax.dynamic_slice_in_dim(key_pad, tile_start, window_span, 0)
            value_window = lax.dynamic_slice_in_dim(value_pad, tile_start, window_span, 0)
            allowed = near & (lax.dynamic_slice_in_dim(valid_pad, tile_start, window_span) > 0)[None, :]
            result, grad_query, grad_key, grad_value = attend(query_tile, grad_tile, key_window, value_window, allowed, HEADS)
            grad_key_acc = lax.dynamic_update_slice_in_dim(grad_key_acc, lax.dynamic_slice_in_dim(grad_key_acc, tile_start, window_span, 0) + grad_key, tile_start, 0)
            grad_value_acc = lax.dynamic_update_slice_in_dim(grad_value_acc, lax.dynamic_slice_in_dim(grad_value_acc, tile_start, window_span, 0) + grad_value, tile_start, 0)
            return (grad_key_acc, grad_value_acc), (result, grad_query)

        def cross_step(carry, tile_index):
            grad_key_acc, grad_value_acc = carry
            tile_start = (tile_index * QT).astype(jnp.int32)
            block_index = (tile_start // BLOCK).astype(jnp.int32)
            band_start = (block_index * BLOCK + offsets[chain, block_index] + HALF).astype(jnp.int32)
            query_tile = lax.dynamic_slice_in_dim(cross_queries[chain], tile_start, QT, 0)
            grad_tile = lax.dynamic_slice_in_dim(grad_out[chain], tile_start, QT, 0)
            key_band = lax.dynamic_slice_in_dim(cross_key_pad, band_start, BLOCK, 0)
            value_band = lax.dynamic_slice_in_dim(cross_value_pad, band_start, BLOCK, 0)
            allowed = (lax.dynamic_slice_in_dim(other_valid, band_start, BLOCK) > 0)[None, :]
            result, grad_query, grad_key, grad_value = attend(query_tile, grad_tile, key_band, value_band, allowed, HEADS)
            grad_key_acc = lax.dynamic_update_slice_in_dim(grad_key_acc, lax.dynamic_slice_in_dim(grad_key_acc, band_start, BLOCK, 0) + grad_key, band_start, 0)
            grad_value_acc = lax.dynamic_update_slice_in_dim(grad_value_acc, lax.dynamic_slice_in_dim(grad_value_acc, band_start, BLOCK, 0) + grad_value, band_start, 0)
            return (grad_key_acc, grad_value_acc), (result, grad_query)

        (self_gk, self_gv), (self_out, self_gq) = lax.scan(self_step, (zeros_pad, zeros_pad), tiles)
        (cross_gk, cross_gv), (cross_out, cross_gq) = lax.scan(cross_step, (zeros_pad, zeros_pad), tiles)
        self_out = self_out.reshape(LEN, -1)
        cross_out = cross_out.reshape(LEN, -1)
        attended = (self_out + cross_out).astype(jnp.bfloat16)
        results.append((attended, self_gq.reshape(LEN, -1).astype(jnp.bfloat16), self_gk[HALF:HALF + LEN].astype(jnp.bfloat16), self_gv[HALF:HALF + LEN].astype(jnp.bfloat16), cross_gq.reshape(LEN, -1).astype(jnp.bfloat16)))
        cross_key_grads[other] = cross_gk[HALF:HALF + LEN].astype(jnp.bfloat16)
        cross_value_grads[other] = cross_gv[HALF:HALF + LEN].astype(jnp.bfloat16)
    stacked = [jnp.stack((results[0][slot], results[1][slot])) for slot in range(5)]
    return (stacked[0], stacked[1], stacked[2], stacked[3], stacked[4], jnp.stack(cross_key_grads), jnp.stack(cross_value_grads))
```

```python
import functools

import jax
import jax.numpy as jnp
from jax import lax
from jax.experimental import pallas as pl
from jax.experimental.pallas import tpu as pltpu
from jax.sharding import PartitionSpec as P

HEADS = 16
HEAD = 64
WINDOW = 2048
TILE = 512
MESH = pl.DeviceIdType.MESH
F32, BF16 = jnp.float32, jnp.bfloat16


def places():
    tower, blk, seq = lax.axis_index("tower"), lax.axis_index("blk"), lax.axis_index("seq")
    peers = dict(
        y=(tower, blk, 1 - seq),
        tower=(1 - tower, blk, seq),
        diag=(1 - tower, blk, 1 - seq),
        low=(tower, blk - 1, seq),
        high=(tower, blk + 1, seq),
    )
    return tower, blk, seq, peers


def greet(blk, blks, peers):
    barrier = pltpu.get_barrier_semaphore()
    for name in ("y", "tower", "diag"):
        pl.semaphore_signal(barrier, inc=1, device_id=peers[name], device_id_type=MESH)

    @pl.when(blk > 0)
    def _():
        pl.semaphore_signal(barrier, inc=1, device_id=peers["low"], device_id_type=MESH)

    @pl.when(blk < blks - 1)
    def _():
        pl.semaphore_signal(barrier, inc=1, device_id=peers["high"], device_id_type=MESH)

    count = 3 + jnp.where(blk > 0, 1, 0) + jnp.where(blk < blks - 1, 1, 0)
    pl.semaphore_wait(barrier, count)


def remote(src, dst, send, recv, device):
    return pltpu.make_async_remote_copy(
        src_ref=src, dst_ref=dst, send_sem=send, recv_sem=recv,
        device_id=device, device_id_type=MESH,
    )


def gather_kernel(
    blks, cols, q_ref, k_ref, v_ref, cq_ref, ck_ref, cv_ref, g_ref, m_ref,
    yk, yv, yq, yg, ycq, part_own, part_y, ymask, low_halo, high_halo, low_mask, high_mask,
    send_sem, recv_sem, low_send, low_recv, high_send, high_recv,
):
    tower, blk, seq, peers = places()
    greet(blk, blks, peers)
    mine = pl.ds(pl.multiple_of(seq * cols, cols), cols)
    theirs = pl.ds(pl.multiple_of((1 - seq) * cols, cols), cols)
    first = [
        remote(m_ref, ymask, send_sem.at[0], recv_sem.at[0], peers["y"]),
        remote(k_ref.at[:, theirs], yk, send_sem.at[1], recv_sem.at[1], peers["y"]),
        remote(v_ref.at[:, theirs], yv, send_sem.at[2], recv_sem.at[2], peers["y"]),
        remote(ck_ref.at[:, theirs], part_y.at[0], send_sem.at[3], recv_sem.at[3], peers["diag"]),
        remote(cv_ref.at[:, theirs], part_y.at[1], send_sem.at[4], recv_sem.at[4], peers["diag"]),
        remote(ck_ref.at[:, mine], part_own.at[0], send_sem.at[5], recv_sem.at[5], peers["tower"]),
        remote(cv_ref.at[:, mine], part_own.at[1], send_sem.at[6], recv_sem.at[6], peers["tower"]),
        remote(q_ref.at[:, theirs], yq, send_sem.at[7], recv_sem.at[7], peers["y"]),
        remote(g_ref.at[:, theirs], yg, send_sem.at[8], recv_sem.at[8], peers["y"]),
        remote(cq_ref.at[:, theirs], ycq, send_sem.at[9], recv_sem.at[9], peers["y"]),
    ]
    own_sources = [k_ref.at[:, mine], v_ref.at[:, mine], part_own.at[0], part_own.at[1], m_ref]
    far_sources = [yk, yv, part_y.at[0], part_y.at[1], ymask]
    own_waits = [None, None, first[5], first[6], None]
    far_waits = [first[1], first[2], first[3], first[4], first[0]]

    def up(sources, at):
        target = high_dst[at]
        return remote(sources[at], target, high_send.at[at], high_recv.at[at], peers["high"])

    def down(sources, at):
        target = low_dst[at]
        return remote(sources[at], target, low_send.at[at], low_recv.at[at], peers["low"])

    high_dst = [low_halo.at[0], low_halo.at[1], low_halo.at[2], low_halo.at[3], low_mask]
    low_dst = [high_halo.at[0], high_halo.at[1], high_halo.at[2], high_halo.at[3], high_mask]
    has_low, has_high = blk > 0, blk < blks - 1
    for copy in first[:5]:
        copy.start()
    first[5].start()
    first[6].start()
    order = (4, 0, 1, 2, 3)
    own_high, own_low = seq == 1, seq == 0
    for copy in first[7:]:
        copy.start()

    def pass_on(sources, waits, pick_high, pick_low):
        for at in order:
            if waits[at] is not None:
                waits[at].wait_recv()

            @pl.when(pick_high & has_high)
            def _():
                up(sources, at).start()

            @pl.when(pick_low & has_low)
            def _():
                down(sources, at).start()

    pass_on(own_sources, own_waits, own_high, own_low)
    pass_on(far_sources, far_waits, own_low, own_high)
    for copy in first[7:]:
        copy.wait_recv()
    for copy in first:
        copy.wait_send()

    @pl.when(has_high)
    def _():
        for at in order:
            up(far_sources, at).wait_send()
            down(far_sources, at).wait_recv()

    @pl.when(has_low)
    def _():
        for at in order:
            down(far_sources, at).wait_send()
            up(far_sources, at).wait_recv()


def attend_kernel(
    blks, rows, cols,
    off_ref, q_ref, k_ref, v_ref, cq_ref, g_ref, m_ref,
    yk, yv, yq, yg, ycq, part_own, part_y, ymask, low_halo, high_halo, low_mask, high_mask,
    y_out, own_out, low_out, high_out, core_out,
    q_s, g_s, cq_s, ext, ext_t, bias, head_t,
):
    tower, blk, seq, _ = places()
    half = rows
    keys = 3 * half
    scale = HEAD ** (-0.5)
    here = pl.ds(pl.multiple_of(seq * half, half), half)
    there = pl.ds(pl.multiple_of((1 - seq) * half, half), half)
    mine = pl.ds(pl.multiple_of(seq * cols, cols), cols)
    ext_here = pl.ds(pl.multiple_of((1 + seq) * half, half), half)
    ext_there = pl.ds(pl.multiple_of((2 - seq) * half, half), half)
    q_s[here, :] = q_ref[:, mine] * BF16(scale)
    q_s[there, :] = yq[...] * BF16(scale)
    cq_s[here, :] = cq_ref[:, mine] * BF16(scale)
    cq_s[there, :] = ycq[...] * BF16(scale)
    g_s[here, :] = g_ref[:, mine]
    g_s[there, :] = yg[...]
    own_sides = [k_ref[:, mine], v_ref[:, mine], part_own[0], part_own[1]]
    far_sides = [yk[...], yv[...], part_y[0], part_y[1]]
    for at in range(4):
        ext[at, ext_here, :] = own_sides[at]
        ext[at, ext_there, :] = far_sides[at]
        ext[at, :half, :] = jnp.where(blk > 0, low_halo[at], jnp.zeros_like(low_halo[at]))
        ext[at, 3 * half :, :] = jnp.where(
            blk < blks - 1, high_halo[at], jnp.zeros_like(high_halo[at])
        )
    for at in range(4):
        ext_t[at] = jnp.transpose(ext[at].astype(F32)).astype(BF16)

    off = off_ref[tower, blk]
    cross_at = pl.multiple_of(jnp.where(off < 0, 0, half), half)
    band_low = off + half

    def column(row):
        wide = jnp.broadcast_to(row.astype(F32), (half, half))
        return jnp.transpose(wide)

    low_ok = jnp.where(blk > 0, 1, 0)
    high_ok = jnp.where(blk < blks - 1, 1, 0)

    def valid_parts(chain):
        at = pl.ds(chain, 1)
        own, far = m_ref[at, :], ymask[at, :]
        first = jnp.where(seq == 0, own, far)
        second = jnp.where(seq == 0, far, own)
        low = jnp.where(low_ok > 0, low_mask[at, :], 0)
        high = jnp.where(high_ok > 0, high_mask[at, :], 0)
        return [column(low), column(first), column(second), column(high)]

    own_valid = valid_parts(tower)
    other_valid = valid_parts(1 - tower)
    row_at = lax.broadcasted_iota(jnp.int32, (half, half), 0)
    col_at = lax.broadcasted_iota(jnp.int32, (half, half), 1)
    for tile in range(2):
        for part in range(3):
            distance = col_at + half - (row_at + part * half)
            near = (jnp.abs(distance) <= half) & (own_valid[tile + part] > 0)
            add = jnp.where(near, 0.0, -1e30)
            bias[tile, part * half : (part + 1) * half, :half] = add
            bias[tile, part * half : (part + 1) * half, half:] = add
    for part in range(3):
        at = row_at + part * half + cross_at
        valid = jnp.where(off < 0, other_valid[part], other_valid[part + 1])
        inside = (at >= band_low) & (at < band_low + 2 * half) & (valid > 0)
        add = jnp.where(inside, 0.0, -1e30)
        bias[2, part * half : (part + 1) * half, :half] = add
        bias[2, part * half : (part + 1) * half, half:] = add

    wide = 2 * HEAD
    lanes = lax.broadcasted_iota(jnp.int32, (half, wide), 1)
    zero = jnp.zeros((half, wide), BF16)

    def split(tile):
        return jnp.concatenate(
            (jnp.where(lanes < HEAD, tile, zero), jnp.where(lanes < HEAD, zero, tile)), 0
        )

    def dot_t(a, b):
        return lax.dot_general(a, b, (((1,), (1,)), ((), ())), preferred_element_type=F32)

    def dot(a, b):
        return jnp.dot(a, b, preferred_element_type=F32)

    def own_heads(both):
        return jnp.concatenate((both[:HEAD, :half], both[HEAD:, half:]), 0)

    def one(pair, query, cot, which, start, add):
        at = pl.ds(pl.multiple_of(pair * wide, wide), wide)
        span = pl.ds(start, keys)
        key = ext[which, span, at]
        value = ext[which + 1, span, at]
        key_t = ext_t[which, at, span]
        value_t = ext_t[which + 1, at, span]
        scores = dot_t(key, query) + bias[add]
        unnormed = jnp.exp(scores - jnp.max(scores, axis=0, keepdims=True))
        weights = unnormed * (1.0 / jnp.sum(unnormed, axis=0, keepdims=True))
        prob = weights.astype(BF16)
        grad_probs = dot_t(value, cot)
        row_dot = jnp.sum(weights * grad_probs, axis=0, keepdims=True)
        grad_scores = (weights * (grad_probs - row_dot)).astype(BF16)
        result = own_heads(dot(value_t, prob))
        grad_query = own_heads(dot(key_t, grad_scores)) * scale
        return result, grad_query, dot(grad_scores, query), dot(prob, cot)

    zero_half = jnp.zeros((half, wide), F32)

    def pair_step(pair, carry):
        at = pl.ds(pl.multiple_of(pair * wide, wide), wide)
        outs = []
        for tile in range(2):
            tile_rows = slice(tile * half, (tile + 1) * half)
            cot = split(g_s[tile_rows, at])
            query = split(q_s[tile_rows, at])
            cross = split(cq_s[tile_rows, at])
            mine_o, mine_q, mine_k, mine_v = one(pair, query, cot, 0, tile * half, tile)
            other_o, other_q, other_k, other_v = one(pair, cross, cot, 2, cross_at, 2)
            head_t[0, at, tile_rows] = mine_o + other_o
            head_t[1, at, tile_rows] = mine_q
            head_t[2, at, tile_rows] = other_q
            outs.append((mine_k, mine_v, other_k, other_v))
        for slot in range(2):
            first, second = outs[0][slot], outs[1][slot]
            low_out[slot, :, at] = first[:half].astype(BF16)
            core_out[slot, 0, :, at] = first[half : 2 * half] + second[:half]
            core_out[slot, 1, :, at] = first[2 * half :] + second[half : 2 * half]
            high_out[slot, :, at] = second[2 * half :].astype(BF16)
        below = off < 0
        for slot in range(2, 4):
            total = outs[0][slot] + outs[1][slot]
            a, b, c = total[:half], total[half : 2 * half], total[2 * half :]
            low_out[slot, :, at] = jnp.where(below, a, zero_half).astype(BF16)
            core_out[slot, 0, :, at] = jnp.where(below, b, a)
            core_out[slot, 1, :, at] = jnp.where(below, c, b)
            high_out[slot, :, at] = jnp.where(below, zero_half, c).astype(BF16)
        return carry

    lax.fori_loop(0, cols // wide, pair_step, 0)
    for slot in range(3):
        whole = jnp.transpose(head_t[slot]).astype(BF16)
        lower, upper = whole[:half], whole[half:]
        own_out[slot] = jnp.where(seq == 0, lower, upper)
        y_out[slot] = jnp.where(seq == 0, upper, lower)


def scatter_kernel(
    blks, cols, y_in, own_in, low_in, high_in, core_in,
    o_out, gq_out, gk_out, gv_out, gcq_out, gck_out, gcv_out,
    recv, y_send, tower_send,
    a_send, a_recv, low_send, low_recv, high_send, high_recv,
):
    tower, blk, seq, peers = places()
    greet(blk, blks, peers)
    mine = pl.ds(pl.multiple_of(seq * cols, cols), cols)
    has_low, has_high = blk > 0, blk < blks - 1
    direct = [o_out, gq_out, gcq_out]
    grads = [gk_out, gv_out, gck_out, gcv_out]

    def down(at):
        return remote(low_in.at[at], recv.at[1, at], low_send.at[at], low_recv.at[at], peers["low"])

    def up(at):
        return remote(high_in.at[at], recv.at[0, at], high_send.at[at], high_recv.at[at], peers["high"])

    def start_down():
        @pl.when(has_low)
        def _():
            for at in range(4):
                down(at).start()

    def start_up():
        @pl.when(has_high)
        def _():
            for at in range(4):
                up(at).start()

    @pl.when(seq == 0)
    def _():
        start_down()
        start_up()

    @pl.when(seq == 1)
    def _():
        start_up()
        start_down()

    sent = [
        remote(y_in.at[at], direct[at].at[:, mine], a_send.at[at], a_recv.at[at], peers["y"])
        for at in range(3)
    ]
    for copy in sent:
        copy.start()
    for at in range(3):
        direct[at][:, mine] = own_in[at]

    @pl.when(blk == 0)
    def _():
        recv[0] = jnp.zeros(recv.shape[1:], BF16)

    @pl.when(blk == blks - 1)
    def _():
        recv[1] = jnp.zeros(recv.shape[1:], BF16)

    def take(low_side, high_side, at):
        @pl.when(low_side & has_low)
        def _():
            up(at).wait_recv()

        @pl.when(high_side & has_high)
        def _():
            down(at).wait_recv()

    for at in range(4):
        take(seq == 1, seq == 0, at)
        y_send[at] = (core_in[at, 1 - seq] + recv[1 - seq, at].astype(F32)).astype(BF16)
        copy = remote(
            y_send.at[at], grads[at].at[:, mine], a_send.at[3 + at], a_recv.at[3 + at],
            peers["y" if at < 2 else "diag"],
        )
        copy.start()
        sent.append(copy)
    for at in (2, 3, 0, 1):
        take(seq == 0, seq == 1, at)
        total = (core_in[at, seq] + recv[seq, at].astype(F32)).astype(BF16)
        if at < 2:
            grads[at][:, mine] = total
        else:
            tower_send[at - 2] = total
            copy = remote(
                tower_send.at[at - 2], grads[at].at[:, mine], a_send.at[5 + at], a_recv.at[5 + at],
                peers["tower"],
            )
            copy.start()
            sent.append(copy)
    for copy in sent:
        copy.wait()

    @pl.when(has_low)
    def _():
        for at in range(4):
            down(at).wait_send()

    @pl.when(has_high)
    def _():
        for at in range(4):
            up(at).wait_send()


def paired(
    queries, key_rows, value_rows, cross_queries, cross_keys, cross_values, grad_out,
    offsets, key_valid,
):
    blks = lax.axis_size("blk")
    heads_here = HEADS // lax.axis_size("seq")
    cols = heads_here * HEAD
    q, k, v, cq, ck, cv, g = (
        value[0] for value in (
            queries, key_rows, value_rows, cross_queries, cross_keys, cross_values, grad_out
        )
    )
    rows = q.shape[0]
    block = 2 * rows
    any_spec = pl.BlockSpec(memory_space=pl.ANY)
    vmem = pl.BlockSpec(memory_space=pltpu.VMEM)
    shape = jax.ShapeDtypeStruct
    side = shape((rows, cols), BF16)
    mask = shape(key_valid.shape, key_valid.dtype)
    dma = pltpu.SemaphoreType.DMA
    gathered = pl.pallas_call(
        functools.partial(gather_kernel, blks, cols),
        out_shape=(
            side, side, side, side, side,
            shape((2, rows, cols), BF16), shape((2, rows, cols), BF16), mask,
            shape((4, rows, cols), BF16), shape((4, rows, cols), BF16), mask, mask,
        ),
        in_specs=[any_spec] * 8,
        out_specs=(any_spec,) * 12,
        scratch_shapes=[dma((10,)), dma((10,)), dma((5,)), dma((5,)), dma((5,)), dma((5,))],
        compiler_params=pltpu.CompilerParams(collective_id=0, has_side_effects=True),
        name="gather_in",
    )(q, k, v, cq, ck, cv, g, key_valid)
    results = pl.pallas_call(
        functools.partial(attend_kernel, blks, rows, cols),
        out_shape=(
            shape((3, rows, cols), BF16), shape((3, rows, cols), BF16),
            shape((4, rows, cols), BF16), shape((4, rows, cols), BF16),
            shape((4, 2, rows, cols), F32),
        ),
        in_specs=[pl.BlockSpec(memory_space=pltpu.SMEM)] + [vmem] * 18,
        out_specs=(vmem,) * 5,
        scratch_shapes=[
            pltpu.VMEM((block, cols), BF16), pltpu.VMEM((block, cols), BF16),
            pltpu.VMEM((block, cols), BF16),
            pltpu.VMEM((4, 2 * block, cols), BF16), pltpu.VMEM((4, cols, 2 * block), BF16),
            pltpu.VMEM((3, 3 * rows, block), F32), pltpu.VMEM((3, cols, block), F32),
        ],
        name="attend",
    )(offsets, q, k, v, cq, g, key_valid, *gathered)
    full = shape((rows, 2 * cols), BF16)
    outs = pl.pallas_call(
        functools.partial(scatter_kernel, blks, cols),
        out_shape=(full,) * 7,
        in_specs=[vmem] * 5,
        out_specs=(vmem,) * 7,
        scratch_shapes=[
            pltpu.VMEM((2, 4, rows, cols), BF16), pltpu.VMEM((4, rows, cols), BF16),
            pltpu.VMEM((2, rows, cols), BF16),
            dma((9,)), dma((9,)), dma((4,)), dma((4,)), dma((4,)), dma((4,)),
        ],
        compiler_params=pltpu.CompilerParams(collective_id=1, has_side_effects=True),
        name="scatter_out",
    )(*results)
    return tuple(piece[None] for piece in outs)


def extended(block, sides, width):
    for axis, dim in sides:
        count = lax.axis_size(axis)
        forward = [(i, i + 1) for i in range(count - 1)]
        backward = [(target, source) for source, target in forward]
        low = lax.ppermute(
            lax.slice_in_dim(block, block.shape[dim] - width, None, axis=dim), axis, forward
        )
        high = lax.ppermute(lax.slice_in_dim(block, 0, width, axis=dim), axis, backward)
        block = jnp.concatenate([low, block, high], axis=dim)
    return block


def swapped(value, axis, bit):
    mask = 2**bit
    pairs = [(source, source ^ mask) for source in range(lax.axis_size(axis))]
    return lax.ppermute(value, axis, pairs)


def passed_along(block, axis, distance):
    devices = range(lax.axis_size(axis))
    route = [(i - distance, i) for i in devices if i - distance in devices]
    return lax.ppermute(block, axis, route)


def attend(query_tile, grad_tile, key_block, value_block, allowed, heads_here):
    score_scale = HEAD ** (-0.5)
    rows_count = query_tile.shape[0]
    keys_count = key_block.shape[0]
    q_heads = query_tile.reshape(rows_count, heads_here, HEAD)
    g_heads = grad_tile.reshape(rows_count, heads_here, HEAD)
    k_heads = key_block.reshape(keys_count, heads_here, HEAD)
    v_heads = value_block.reshape(keys_count, heads_here, HEAD)
    scores = (
        jnp.einsum("qhe,khe->hqk", q_heads, k_heads, preferred_element_type=jnp.float32)
        * score_scale
    )
    scores = jnp.where(allowed[None], scores, -1e30)
    row_max = jnp.max(scores, axis=2)
    unnormed = jnp.exp(scores - row_max[:, :, None])
    row_sum = jnp.sum(unnormed, axis=2)
    weights = unnormed / row_sum[:, :, None]
    prob_bf = weights.astype(jnp.bfloat16)
    result = jnp.einsum(
        "hqk,khe->qhe", prob_bf, v_heads, preferred_element_type=jnp.float32
    ).reshape(rows_count, -1)
    grad_probs = jnp.einsum("qhe,khe->hqk", g_heads, v_heads, preferred_element_type=jnp.float32)
    row_dot = jnp.sum(weights * grad_probs, axis=2)
    grad_scores = (weights * (grad_probs - row_dot[:, :, None]) * score_scale).astype(jnp.bfloat16)
    grad_query = jnp.einsum(
        "hqk,khe->qhe", grad_scores, k_heads, preferred_element_type=jnp.float32
    ).reshape(rows_count, -1)
    grad_key = jnp.einsum(
        "hqk,qhe->khe", grad_scores, q_heads, preferred_element_type=jnp.float32
    ).reshape(keys_count, -1)
    grad_value = jnp.einsum(
        "hqk,qhe->khe", prob_bf, g_heads, preferred_element_type=jnp.float32
    ).reshape(keys_count, -1)
    return (result, grad_query, grad_key, grad_value, jnp.stack((row_max, row_sum, row_dot)))


def shards(
    queries,
    key_rows,
    value_rows,
    cross_queries,
    cross_keys,
    cross_values,
    grad_out,
    offsets,
    key_valid,
):
    seq_count = lax.axis_size("seq")
    heads_here = HEADS // seq_count
    local_rows = (
        queries[0],
        key_rows[0],
        value_rows[0],
        cross_queries[0],
        cross_keys[0],
        cross_values[0],
        grad_out[0],
    )
    query_here, key_here, value_here, cross_query, cross_key, cross_value, cotangent = (
        lax.all_to_all(local_rows[0], "seq", split_axis=1, concat_axis=0, tiled=True),
        lax.all_to_all(local_rows[1], "seq", split_axis=1, concat_axis=0, tiled=True),
        lax.all_to_all(local_rows[2], "seq", split_axis=1, concat_axis=0, tiled=True),
        lax.all_to_all(local_rows[3], "seq", split_axis=1, concat_axis=0, tiled=True),
        lax.all_to_all(local_rows[4], "seq", split_axis=1, concat_axis=0, tiled=True),
        lax.all_to_all(local_rows[5], "seq", split_axis=1, concat_axis=0, tiled=True),
        lax.all_to_all(local_rows[6], "seq", split_axis=1, concat_axis=0, tiled=True),
    )
    block_len = query_here.shape[0]
    columns = query_here.shape[1]
    half_width = min(WINDOW // 2, block_len // 2)
    tile_rows = min(TILE, block_len)
    tile_count = block_len // tile_rows
    window_span = tile_rows + 2 * half_width
    tower_id = lax.axis_index("tower")
    block_id = lax.axis_index("blk")
    block_mask = lax.all_gather(key_valid, "seq", axis=1, tiled=True)
    mask_ext = extended(block_mask, (("blk", 1),), half_width)
    self_valid = lax.dynamic_index_in_dim(mask_ext, tower_id, 0, keepdims=False)
    other_valid = lax.dynamic_index_in_dim(mask_ext, 1 - tower_id, 0, keepdims=False)
    pair_ext = extended(jnp.stack((key_here, value_here)), (("blk", 1),), half_width)
    partner = swapped(jnp.stack((cross_key, cross_value)), "tower", 0)
    partner_ext = extended(partner, (("blk", 1),), half_width)
    align_shift = offsets[tower_id, block_id]
    band_start = half_width + align_shift
    band = lax.dynamic_slice_in_dim(partner_ext, band_start, block_len, 1)
    band_valid = lax.dynamic_slice_in_dim(other_valid, band_start, block_len) > 0
    rows_local = jnp.arange(tile_rows)
    keys_local = jnp.arange(window_span)
    near = jnp.abs(rows_local[:, None] + half_width - keys_local[None, :]) <= half_width

    def self_step(carry, tile_index):
        grad_key_acc, grad_value_acc = carry
        tile_start = tile_index * tile_rows
        query_tile = lax.dynamic_slice_in_dim(query_here, tile_start, tile_rows, 0)
        grad_tile = lax.dynamic_slice_in_dim(cotangent, tile_start, tile_rows, 0)
        key_window = lax.dynamic_slice_in_dim(pair_ext[0], tile_start, window_span, 0)
        value_window = lax.dynamic_slice_in_dim(pair_ext[1], tile_start, window_span, 0)
        allowed = (
            near & (lax.dynamic_slice_in_dim(self_valid, tile_start, window_span) > 0)[None, :]
        )
        result, grad_query, grad_key, grad_value, stats = attend(
            query_tile, grad_tile, key_window, value_window, allowed, heads_here
        )
        grad_key_acc = lax.dynamic_update_slice_in_dim(
            grad_key_acc,
            lax.dynamic_slice_in_dim(grad_key_acc, tile_start, window_span, 0) + grad_key,
            tile_start,
            0,
        )
        grad_value_acc = lax.dynamic_update_slice_in_dim(
            grad_value_acc,
            lax.dynamic_slice_in_dim(grad_value_acc, tile_start, window_span, 0) + grad_value,
            tile_start,
            0,
        )
        return ((grad_key_acc, grad_value_acc), (result, grad_query, stats))

    def cross_step(carry, tile_index):
        grad_key_acc, grad_value_acc = carry
        tile_start = tile_index * tile_rows
        query_tile = lax.dynamic_slice_in_dim(cross_query, tile_start, tile_rows, 0)
        grad_tile = lax.dynamic_slice_in_dim(cotangent, tile_start, tile_rows, 0)
        result, grad_query, grad_key, grad_value, stats = attend(
            query_tile, grad_tile, band[0], band[1], band_valid[None, :], heads_here
        )
        return ((grad_key_acc + grad_key, grad_value_acc + grad_value), (result, grad_query))

    zeros_ext = jnp.zeros((block_len + 2 * half_width, columns), jnp.float32)
    zeros_band = jnp.zeros((block_len, columns), jnp.float32)
    tile_ids = jnp.arange(tile_count)
    (self_gk, self_gv), (self_out, self_gq, self_stats) = lax.scan(
        self_step, (zeros_ext, zeros_ext), tile_ids
    )
    (cross_gk, cross_gv), (cross_out, cross_gq) = lax.scan(
        cross_step, (zeros_band, zeros_band), tile_ids
    )
    self_out = self_out.reshape(block_len, columns)
    cross_out = cross_out.reshape(block_len, columns)
    self_stats = jnp.transpose(self_stats, (1, 2, 0, 3)).reshape(3, heads_here, block_len)
    attended = (self_out + cross_out).astype(jnp.bfloat16)
    cross_ext = jnp.zeros((2, block_len + 2 * half_width, columns), jnp.float32)
    cross_ext = lax.dynamic_update_slice_in_dim(
        cross_ext, jnp.stack((cross_gk, cross_gv)), band_start, 1
    )
    self_ext = jnp.stack((self_gk, self_gv))
    self_core = self_ext[:, half_width : half_width + block_len]
    cross_core = cross_ext[:, half_width : half_width + block_len]
    upper_cut = block_len - half_width
    lower_send = jnp.concatenate((self_ext[:, :half_width], cross_ext[:, :half_width]), 0)
    upper_send = jnp.concatenate(
        (self_ext[:, block_len + half_width :], cross_ext[:, block_len + half_width :]), 0
    )
    from_above = passed_along(lower_send.astype(jnp.bfloat16), "blk", -1).astype(lower_send.dtype)
    from_below = passed_along(upper_send.astype(jnp.bfloat16), "blk", 1).astype(upper_send.dtype)
    self_core = (
        self_core.at[:, upper_cut:].add(from_above[:2]).at[:, :half_width].add(from_below[:2])
    )
    cross_core = (
        cross_core.at[:, upper_cut:].add(from_above[2:]).at[:, :half_width].add(from_below[2:])
    )
    returned = swapped(cross_core.astype(jnp.bfloat16), "tower", 0)
    head_outs = (
        attended,
        self_gq.reshape(block_len, columns).astype(jnp.bfloat16),
        self_core[0].astype(jnp.bfloat16),
        self_core[1].astype(jnp.bfloat16),
        cross_gq.reshape(block_len, columns).astype(jnp.bfloat16),
        returned[0],
        returned[1],
    )
    token_outs = (
        lax.all_to_all(head_outs[0], "seq", split_axis=0, concat_axis=1, tiled=True),
        lax.all_to_all(head_outs[1], "seq", split_axis=0, concat_axis=1, tiled=True),
        lax.all_to_all(head_outs[2], "seq", split_axis=0, concat_axis=1, tiled=True),
        lax.all_to_all(head_outs[3], "seq", split_axis=0, concat_axis=1, tiled=True),
        lax.all_to_all(head_outs[4], "seq", split_axis=0, concat_axis=1, tiled=True),
        lax.all_to_all(head_outs[5], "seq", split_axis=0, concat_axis=1, tiled=True),
        lax.all_to_all(head_outs[6], "seq", split_axis=0, concat_axis=1, tiled=True),
    )
    return tuple((piece[None] for piece in token_outs))


def solution(mesh):
    in_specs = (
        P("tower", ("blk", "seq"), None),
        P("tower", ("blk", "seq"), None),
        P("tower", ("blk", "seq"), None),
        P("tower", ("blk", "seq"), None),
        P("tower", ("blk", "seq"), None),
        P("tower", ("blk", "seq"), None),
        P("tower", ("blk", "seq"), None),
        P(),
        P(None, ("blk", "seq")),
    )
    out_specs = (
        P("tower", ("blk", "seq"), None),
        P("tower", ("blk", "seq"), None),
        P("tower", ("blk", "seq"), None),
        P("tower", ("blk", "seq"), None),
        P("tower", ("blk", "seq"), None),
        P("tower", ("blk", "seq"), None),
        P("tower", ("blk", "seq"), None),
    )
    body = paired if mesh.shape["seq"] == 2 else shards
    return jax.shard_map(body, mesh=mesh, in_specs=in_specs, out_specs=out_specs, check_vma=False)
```

```python
import functools

import jax
import jax.numpy as jnp
from jax import lax
from jax.experimental import pallas as pl
from jax.experimental.pallas import tpu as pltpu
from jax.sharding import PartitionSpec as P

HEADS = 16
HEAD = 64
WINDOW = 2048
TILE = 512
MESH = pl.DeviceIdType.MESH
F32, BF16 = jnp.float32, jnp.bfloat16


def places():
    tower, blk, seq = lax.axis_index("tower"), lax.axis_index("blk"), lax.axis_index("seq")
    peers = dict(
        y=(tower, blk, 1 - seq),
        tower=(1 - tower, blk, seq),
        diag=(1 - tower, blk, 1 - seq),
        low=(tower, blk - 1, seq),
        high=(tower, blk + 1, seq),
    )
    return tower, blk, seq, peers


def greet(blk, blks, peers):
    barrier = pltpu.get_barrier_semaphore()
    for name in ("y", "tower", "diag"):
        pl.semaphore_signal(barrier, inc=1, device_id=peers[name], device_id_type=MESH)

    @pl.when(blk > 0)
    def _():
        pl.semaphore_signal(barrier, inc=1, device_id=peers["low"], device_id_type=MESH)

    @pl.when(blk < blks - 1)
    def _():
        pl.semaphore_signal(barrier, inc=1, device_id=peers["high"], device_id_type=MESH)

    count = 3 + jnp.where(blk > 0, 1, 0) + jnp.where(blk < blks - 1, 1, 0)
    pl.semaphore_wait(barrier, count)


def remote(src, dst, send, recv, device):
    return pltpu.make_async_remote_copy(
        src_ref=src, dst_ref=dst, send_sem=send, recv_sem=recv,
        device_id=device, device_id_type=MESH,
    )


def fused_kernel(
    blks, rows, cols,
    off_ref, q_ref, k_ref, v_ref, cq_ref, ck_ref, cv_ref, g_ref, m_ref,
    o_out, gq_out, gk_out, gv_out, gcq_out, gck_out, gcv_out,
    side, ext, mask_ext, bias, y_stage, t_stage, low_stage, high_stage, core, recv,
    local_sem, mask_send, mask_recv, in_send, in_recv,
    low_send, low_recv, high_send, high_recv,
    out_send, out_recv, glow_send, glow_recv, ghigh_send, ghigh_recv,
):
    tower, blk, seq, peers = places()
    half, wide = rows, 2 * HEAD
    keys, groups = 3 * rows, cols // (2 * HEAD)
    scale = HEAD ** (-0.5)
    has_low, has_high = blk > 0, blk < blks - 1
    here = pl.ds(pl.multiple_of(seq * half, half), half)
    ext_here = pl.ds(pl.multiple_of((1 + seq) * half, half), half)
    mine = pl.ds(pl.multiple_of(seq * cols, cols), cols)
    inner_low, inner_high = pl.ds(half, half), pl.ds(2 * half, half)
    outer_low, outer_high = pl.ds(0, half), pl.ds(3 * half, half)
    direct = [o_out, gq_out, gcq_out]
    grads = [gk_out, gv_out, gck_out, gcv_out]

    def strip(g, base=0):
        return pl.ds(pl.multiple_of(base + g * wide, wide), wide)

    def incoming(g):
        at = strip(g)
        keep, give = strip(g, seq * cols), strip(g, (1 - seq) * cols)
        moves = [
            (k_ref.at[:, give], ext.at[0, ext_here, at], "y"),
            (v_ref.at[:, give], ext.at[1, ext_here, at], "y"),
            (ck_ref.at[:, give], ext.at[2, ext_here, at], "diag"),
            (cv_ref.at[:, give], ext.at[3, ext_here, at], "diag"),
            (ck_ref.at[:, keep], ext.at[2, ext_here, at], "tower"),
            (cv_ref.at[:, keep], ext.at[3, ext_here, at], "tower"),
            (q_ref.at[:, give], side.at[0, here, at], "y"),
            (g_ref.at[:, give], side.at[2, here, at], "y"),
            (cq_ref.at[:, give], side.at[1, here, at], "y"),
        ]
        return [
            remote(src, dst, in_send.at[g, i], in_recv.at[g, i], peers[to])
            for i, (src, dst, to) in enumerate(moves)
        ]

    def up(g, i):
        at = strip(g)
        return remote(
            ext.at[i, inner_high, at], ext.at[i, outer_low, at],
            high_send.at[g, i], high_recv.at[g, i], peers["high"],
        )

    def down(g, i):
        at = strip(g)
        return remote(
            ext.at[i, inner_low, at], ext.at[i, outer_high, at],
            low_send.at[g, i], low_recv.at[g, i], peers["low"],
        )

    mask_y = remote(m_ref, mask_ext.at[1 + seq], mask_send.at[0], mask_recv.at[0], peers["y"])
    mask_up = remote(mask_ext.at[2], mask_ext.at[0], mask_send.at[1], mask_recv.at[1], peers["high"])
    mask_down = remote(mask_ext.at[1], mask_ext.at[3], mask_send.at[2], mask_recv.at[2], peers["low"])

    def pass_on(g, own):
        moved = incoming(g)
        to_high = (seq == 1) if own else (seq == 0)
        to_low = (seq == 0) if own else (seq == 1)
        for i in range(4):
            if not own:
                moved[i].wait_recv()
            elif i >= 2:
                moved[i + 2].wait_recv()

            @pl.when(to_high & has_high)
            def _():
                up(g, i).start()

            @pl.when(to_low & has_low)
            def _():
                down(g, i).start()

    locals_ = [
        pltpu.make_async_copy(k_ref.at[:, mine], ext.at[0, ext_here, :], local_sem.at[0]),
        pltpu.make_async_copy(v_ref.at[:, mine], ext.at[1, ext_here, :], local_sem.at[1]),
        pltpu.make_async_copy(m_ref, mask_ext.at[1 + seq], local_sem.at[2]),
        pltpu.make_async_copy(q_ref.at[:, mine], side.at[0, here, :], local_sem.at[3]),
        pltpu.make_async_copy(cq_ref.at[:, mine], side.at[1, here, :], local_sem.at[4]),
        pltpu.make_async_copy(g_ref.at[:, mine], side.at[2, here, :], local_sem.at[5]),
    ]
    for copy in locals_:
        copy.start()

    @pl.when(blk == 0)
    def _():
        ext[:, :half, :] = jnp.zeros((4, half, cols), BF16)
        mask_ext[0] = jnp.zeros(mask_ext.shape[1:], jnp.int32)
        recv[0] = jnp.zeros(recv.shape[1:], BF16)

    @pl.when(blk == blks - 1)
    def _():
        ext[:, 3 * half :, :] = jnp.zeros((4, half, cols), BF16)
        mask_ext[3] = jnp.zeros(mask_ext.shape[1:], jnp.int32)
        recv[1] = jnp.zeros(recv.shape[1:], BF16)

    greet(blk, blks, peers)
    mask_y.start()
    for g in range(groups + 1):
        if g < groups:
            for copy in incoming(g)[:6]:
                copy.start()
        if g > 0:
            for copy in incoming(g - 1)[6:]:
                copy.start()
    for copy in locals_:
        copy.wait()
    pass_on(0, True)
    mask_y.wait_recv()

    @pl.when(has_high)
    def _():
        mask_up.start()

    @pl.when(has_low)
    def _():
        mask_down.start()

    pass_on(0, False)
    if groups > 1:
        pass_on(1, True)

    @pl.when(has_high)
    def _():
        mask_down.wait_recv()

    @pl.when(has_low)
    def _():
        mask_up.wait_recv()

    off = off_ref[tower, blk]
    below = off < 0
    cross_at = jnp.where(below, 0, half)
    band_low = off + half

    def column(part, chain):
        row = jnp.where(
            chain == 0, mask_ext[part, 0:1, :].astype(F32), mask_ext[part, 1:2, :].astype(F32)
        )
        return jnp.transpose(jnp.broadcast_to(row, (half, half)))

    own_valid = [column(part, tower) for part in range(4)]
    other_valid = [column(part, 1 - tower) for part in range(4)]
    row_at = lax.broadcasted_iota(jnp.int32, (half, half), 0)
    col_at = lax.broadcasted_iota(jnp.int32, (half, half), 1)
    for part in range(3):
        where = slice(part * half, (part + 1) * half)
        distance = col_at + half - (row_at + part * half)
        for tile in range(2):
            near = (jnp.abs(distance) <= half) & (own_valid[tile + part] > 0)
            add = jnp.where(near, 0.0, -1e30)
            bias[tile, where, :half] = add
            bias[tile, where, half:] = add
        at = row_at + part * half + cross_at
        valid = jnp.where(below, other_valid[part], other_valid[part + 1])
        inside = (at >= band_low) & (at < band_low + 2 * half) & (valid > 0)
        add = jnp.where(inside, 0.0, -1e30)
        bias[2, where, :half] = add
        bias[2, where, half:] = add

    lanes = lax.broadcasted_iota(jnp.int32, (half, wide), 1)
    zero = jnp.zeros((half, wide), BF16)
    zero_half = jnp.zeros((half, wide), F32)

    def split(tile):
        return jnp.concatenate(
            (jnp.where(lanes < HEAD, tile, zero), jnp.where(lanes < HEAD, zero, tile)), 0
        )

    def dot_t(a, b):
        return lax.dot_general(a, b, (((1,), (1,)), ((), ())), preferred_element_type=F32)

    def dot(a, b):
        return jnp.dot(a, b, preferred_element_type=F32)

    def own_heads(both):
        return jnp.concatenate((both[:HEAD, :half], both[HEAD:, half:]), 0)

    def turned(x):
        return jnp.transpose(x.astype(F32)).astype(BF16)

    def one(query, cot, key, value, key_t, value_t, add):
        scores = dot_t(key, query) + bias[add]
        unnormed = jnp.exp(scores - jnp.max(scores, axis=0, keepdims=True))
        weights = unnormed * (1.0 / jnp.sum(unnormed, axis=0, keepdims=True))
        prob = weights.astype(BF16)
        grad_probs = dot_t(value, cot)
        row_dot = jnp.sum(weights * grad_probs, axis=0, keepdims=True)
        grad_scores = (weights * (grad_probs - row_dot)).astype(BF16)
        result = own_heads(dot(value_t, prob))
        grad_query = own_heads(dot(key_t, grad_scores)) * scale
        return result, grad_query, dot(grad_scores, query), dot(prob, cot)

    def compute(g):
        at = strip(g)
        key, value = ext[0, :, at], ext[1, :, at]
        ckey = jnp.where(below, ext[2, :keys, at], ext[2, half:, at])
        cvalue = jnp.where(below, ext[3, :keys, at], ext[3, half:, at])
        key_t, value_t, ckey_t, cvalue_t = turned(key), turned(value), turned(ckey), turned(cvalue)
        grad_parts, head_parts = [], []
        for tile in range(2):
            span = slice(tile * half, tile * half + keys)
            part = slice(tile * half, (tile + 1) * half)
            cot = split(side[2, part, at])
            query = split(side[0, part, at] * BF16(scale))
            cross = split(side[1, part, at] * BF16(scale))
            so, sq, sk, sv = one(
                query, cot, key[span], value[span], key_t[:, span], value_t[:, span], tile
            )
            co, cq, ck, cv = one(cross, cot, ckey, cvalue, ckey_t, cvalue_t, 2)
            head_parts.append((so + co, sq, cq))
            grad_parts.append((sk, sv, ck, cv))
        for i in range(2):
            first, second = grad_parts[0][i], grad_parts[1][i]
            low_stage[i, :, at] = first[:half].astype(BF16)
            core[i, 0, :, at] = first[half : 2 * half] + second[:half]
            core[i, 1, :, at] = first[2 * half :] + second[half : 2 * half]
            high_stage[i, :, at] = second[2 * half :].astype(BF16)
        for i in range(2, 4):
            total = grad_parts[0][i] + grad_parts[1][i]
            a, b, c = total[:half], total[half : 2 * half], total[2 * half :]
            low_stage[i, :, at] = jnp.where(below, a, zero_half).astype(BF16)
            core[i, 0, :, at] = jnp.where(below, b, a)
            core[i, 1, :, at] = jnp.where(below, c, b)
            high_stage[i, :, at] = jnp.where(below, zero_half, c).astype(BF16)
        for i in range(3):
            lower = turned(head_parts[0][i])
            upper = turned(head_parts[1][i])
            direct[i][:, strip(g, seq * cols)] = jnp.where(seq == 0, lower, upper)
            y_stage[i, :, at] = jnp.where(seq == 0, upper, lower)

    def grad_down(g, i):
        at = strip(g)
        return remote(
            low_stage.at[i, :, at], recv.at[1, i, :, at],
            glow_send.at[g, i], glow_recv.at[g, i], peers["low"],
        )

    def grad_up(g, i):
        at = strip(g)
        return remote(
            high_stage.at[i, :, at], recv.at[0, i, :, at],
            ghigh_send.at[g, i], ghigh_recv.at[g, i], peers["high"],
        )

    def outgoing(g):
        at, to_at = strip(g), strip(g, seq * cols)
        moves = [(y_stage.at[i, :, at], direct[i].at[:, to_at], "y") for i in range(3)]
        moves += [
            (y_stage.at[3 + i, :, at], grads[i].at[:, to_at], "y" if i < 2 else "diag")
            for i in range(4)
        ]
        moves += [(t_stage.at[i, :, at], grads[2 + i].at[:, to_at], "tower") for i in range(2)]
        return [
            remote(src, dst, out_send.at[g, i], out_recv.at[g, i], peers[to])
            for i, (src, dst, to) in enumerate(moves)
        ]

    def start_down(g):
        @pl.when(has_low)
        def _():
            for i in range(4):
                grad_down(g, i).start()

    def start_up(g):
        @pl.when(has_high)
        def _():
            for i in range(4):
                grad_up(g, i).start()

    def give(g):
        @pl.when(seq == 0)
        def _():
            start_down(g)
            start_up(g)

        @pl.when(seq == 1)
        def _():
            start_up(g)
            start_down(g)

        for copy in outgoing(g)[:3]:
            copy.start()

    def finish(g):
        at = strip(g)
        moves = outgoing(g)

        def take(low_side, high_side, i):
            @pl.when(low_side & has_low)
            def _():
                grad_up(g, i).wait_recv()

            @pl.when(high_side & has_high)
            def _():
                grad_down(g, i).wait_recv()

        for i in range(4):
            take(seq == 1, seq == 0, i)
            y_stage[3 + i, :, at] = (
                core[i, 1 - seq, :, at] + recv[1 - seq, i, :, at].astype(F32)
            ).astype(BF16)
            moves[3 + i].start()
        for i in (2, 3, 0, 1):
            take(seq == 0, seq == 1, i)
            total = (core[i, seq, :, at] + recv[seq, i, :, at].astype(F32)).astype(BF16)
            if i < 2:
                grads[i][:, strip(g, seq * cols)] = total
            else:
                t_stage[i - 2, :, at] = total
                moves[5 + i].start()

    def step(g, carry):
        @pl.when(g + 1 < groups)
        def _():
            pass_on(g + 1, False)

        @pl.when(g + 2 < groups)
        def _():
            pass_on(g + 2, True)

        for copy in incoming(g)[6:]:
            copy.wait_recv()

        @pl.when(has_high)
        def _():
            for i in range(4):
                down(g, i).wait_recv()

        @pl.when(has_low)
        def _():
            for i in range(4):
                up(g, i).wait_recv()

        compute(g)
        give(g)

        @pl.when(g > 0)
        def _():
            finish(g - 1)

        return carry

    lax.fori_loop(0, groups, step, 0)
    finish(groups - 1)

    def close(g, carry):
        for copy in incoming(g):
            copy.wait_send()
        for copy in outgoing(g):
            copy.wait()

        @pl.when(has_high)
        def _():
            for i in range(4):
                up(g, i).wait_send()
                grad_up(g, i).wait_send()

        @pl.when(has_low)
        def _():
            for i in range(4):
                down(g, i).wait_send()
                grad_down(g, i).wait_send()

        return carry

    lax.fori_loop(0, groups, close, 0)
    mask_y.wait_send()

    @pl.when(has_high)
    def _():
        mask_up.wait_send()

    @pl.when(has_low)
    def _():
        mask_down.wait_send()


def copy_kernel(*refs):
    count = len(refs) // 2
    for src, dst in zip(refs[:count], refs[count:]):
        dst[...] = src[...]


def paired(
    queries, key_rows, value_rows, cross_queries, cross_keys, cross_values, grad_out,
    offsets, key_valid,
):
    blks = lax.axis_size("blk")
    cols = HEADS // lax.axis_size("seq") * HEAD
    values = [
        value[0] for value in (
            queries, key_rows, value_rows, cross_queries, cross_keys, cross_values, grad_out
        )
    ]
    rows = queries.shape[1]
    block, groups = 2 * rows, cols // (2 * HEAD)
    vmem = pl.BlockSpec(memory_space=pltpu.VMEM)
    dma = pltpu.SemaphoreType.DMA
    full = jax.ShapeDtypeStruct((rows, 2 * cols), BF16)
    outs = pl.pallas_call(
        functools.partial(fused_kernel, blks, rows, cols),
        out_shape=(full,) * 7,
        in_specs=[pl.BlockSpec(memory_space=pltpu.SMEM)] + [pl.BlockSpec(memory_space=pl.ANY)] * 8,
        out_specs=(vmem,) * 7,
        scratch_shapes=[
            pltpu.VMEM((3, block, cols), BF16),
            pltpu.VMEM((4, 2 * block, cols), BF16),
            pltpu.VMEM((4,) + key_valid.shape, jnp.int32),
            pltpu.VMEM((3, 3 * rows, block), F32),
            pltpu.VMEM((7, rows, cols), BF16),
            pltpu.VMEM((2, rows, cols), BF16),
            pltpu.VMEM((4, rows, cols), BF16),
            pltpu.VMEM((4, rows, cols), BF16),
            pltpu.VMEM((4, 2, rows, cols), F32),
            pltpu.VMEM((2, 4, rows, cols), BF16),
            dma((6,)), dma((3,)), dma((3,)),
            dma((groups, 9)), dma((groups, 9)),
            dma((groups, 4)), dma((groups, 4)), dma((groups, 4)), dma((groups, 4)),
            dma((groups, 9)), dma((groups, 9)),
            dma((groups, 4)), dma((groups, 4)), dma((groups, 4)), dma((groups, 4)),
        ],
        compiler_params=pltpu.CompilerParams(collective_id=0, has_side_effects=True),
        name="attend_pairs",
    )(offsets, *values, key_valid)
    outs = pl.pallas_call(
        copy_kernel,
        out_shape=(full,) * 7,
        in_specs=[vmem] * 7,
        out_specs=(vmem,) * 7,
        name="hand_over",
    )(*outs)
    return tuple(piece[None] for piece in outs)


def extended(block, sides, width):
    for axis, dim in sides:
        count = lax.axis_size(axis)
        forward = [(i, i + 1) for i in range(count - 1)]
        backward = [(target, source) for source, target in forward]
        low = lax.ppermute(
            lax.slice_in_dim(block, block.shape[dim] - width, None, axis=dim), axis, forward
        )
        high = lax.ppermute(lax.slice_in_dim(block, 0, width, axis=dim), axis, backward)
        block = jnp.concatenate([low, block, high], axis=dim)
    return block


def swapped(value, axis, bit):
    mask = 2**bit
    pairs = [(source, source ^ mask) for source in range(lax.axis_size(axis))]
    return lax.ppermute(value, axis, pairs)


def passed_along(block, axis, distance):
    devices = range(lax.axis_size(axis))
    route = [(i - distance, i) for i in devices if i - distance in devices]
    return lax.ppermute(block, axis, route)


def attend(query_tile, grad_tile, key_block, value_block, allowed, heads_here):
    score_scale = HEAD ** (-0.5)
    rows_count = query_tile.shape[0]
    keys_count = key_block.shape[0]
    q_heads = query_tile.reshape(rows_count, heads_here, HEAD)
    g_heads = grad_tile.reshape(rows_count, heads_here, HEAD)
    k_heads = key_block.reshape(keys_count, heads_here, HEAD)
    v_heads = value_block.reshape(keys_count, heads_here, HEAD)
    scores = (
        jnp.einsum("qhe,khe->hqk", q_heads, k_heads, preferred_element_type=jnp.float32)
        * score_scale
    )
    scores = jnp.where(allowed[None], scores, -1e30)
    row_max = jnp.max(scores, axis=2)
    unnormed = jnp.exp(scores - row_max[:, :, None])
    row_sum = jnp.sum(unnormed, axis=2)
    weights = unnormed / row_sum[:, :, None]
    prob_bf = weights.astype(jnp.bfloat16)
    result = jnp.einsum(
        "hqk,khe->qhe", prob_bf, v_heads, preferred_element_type=jnp.float32
    ).reshape(rows_count, -1)
    grad_probs = jnp.einsum("qhe,khe->hqk", g_heads, v_heads, preferred_element_type=jnp.float32)
    row_dot = jnp.sum(weights * grad_probs, axis=2)
    grad_scores = (weights * (grad_probs - row_dot[:, :, None]) * score_scale).astype(jnp.bfloat16)
    grad_query = jnp.einsum(
        "hqk,khe->qhe", grad_scores, k_heads, preferred_element_type=jnp.float32
    ).reshape(rows_count, -1)
    grad_key = jnp.einsum(
        "hqk,qhe->khe", grad_scores, q_heads, preferred_element_type=jnp.float32
    ).reshape(keys_count, -1)
    grad_value = jnp.einsum(
        "hqk,qhe->khe", prob_bf, g_heads, preferred_element_type=jnp.float32
    ).reshape(keys_count, -1)
    return (result, grad_query, grad_key, grad_value, jnp.stack((row_max, row_sum, row_dot)))


def shards(
    queries,
    key_rows,
    value_rows,
    cross_queries,
    cross_keys,
    cross_values,
    grad_out,
    offsets,
    key_valid,
):
    seq_count = lax.axis_size("seq")
    heads_here = HEADS // seq_count
    local_rows = (
        queries[0],
        key_rows[0],
        value_rows[0],
        cross_queries[0],
        cross_keys[0],
        cross_values[0],
        grad_out[0],
    )
    query_here, key_here, value_here, cross_query, cross_key, cross_value, cotangent = (
        lax.all_to_all(local_rows[0], "seq", split_axis=1, concat_axis=0, tiled=True),
        lax.all_to_all(local_rows[1], "seq", split_axis=1, concat_axis=0, tiled=True),
        lax.all_to_all(local_rows[2], "seq", split_axis=1, concat_axis=0, tiled=True),
        lax.all_to_all(local_rows[3], "seq", split_axis=1, concat_axis=0, tiled=True),
        lax.all_to_all(local_rows[4], "seq", split_axis=1, concat_axis=0, tiled=True),
        lax.all_to_all(local_rows[5], "seq", split_axis=1, concat_axis=0, tiled=True),
        lax.all_to_all(local_rows[6], "seq", split_axis=1, concat_axis=0, tiled=True),
    )
    block_len = query_here.shape[0]
    columns = query_here.shape[1]
    half_width = min(WINDOW // 2, block_len // 2)
    tile_rows = min(TILE, block_len)
    tile_count = block_len // tile_rows
    window_span = tile_rows + 2 * half_width
    tower_id = lax.axis_index("tower")
    block_id = lax.axis_index("blk")
    block_mask = lax.all_gather(key_valid, "seq", axis=1, tiled=True)
    mask_ext = extended(block_mask, (("blk", 1),), half_width)
    self_valid = lax.dynamic_index_in_dim(mask_ext, tower_id, 0, keepdims=False)
    other_valid = lax.dynamic_index_in_dim(mask_ext, 1 - tower_id, 0, keepdims=False)
    pair_ext = extended(jnp.stack((key_here, value_here)), (("blk", 1),), half_width)
    partner = swapped(jnp.stack((cross_key, cross_value)), "tower", 0)
    partner_ext = extended(partner, (("blk", 1),), half_width)
    align_shift = offsets[tower_id, block_id]
    band_start = half_width + align_shift
    band = lax.dynamic_slice_in_dim(partner_ext, band_start, block_len, 1)
    band_valid = lax.dynamic_slice_in_dim(other_valid, band_start, block_len) > 0
    rows_local = jnp.arange(tile_rows)
    keys_local = jnp.arange(window_span)
    near = jnp.abs(rows_local[:, None] + half_width - keys_local[None, :]) <= half_width

    def self_step(carry, tile_index):
        grad_key_acc, grad_value_acc = carry
        tile_start = tile_index * tile_rows
        query_tile = lax.dynamic_slice_in_dim(query_here, tile_start, tile_rows, 0)
        grad_tile = lax.dynamic_slice_in_dim(cotangent, tile_start, tile_rows, 0)
        key_window = lax.dynamic_slice_in_dim(pair_ext[0], tile_start, window_span, 0)
        value_window = lax.dynamic_slice_in_dim(pair_ext[1], tile_start, window_span, 0)
        allowed = (
            near & (lax.dynamic_slice_in_dim(self_valid, tile_start, window_span) > 0)[None, :]
        )
        result, grad_query, grad_key, grad_value, stats = attend(
            query_tile, grad_tile, key_window, value_window, allowed, heads_here
        )
        grad_key_acc = lax.dynamic_update_slice_in_dim(
            grad_key_acc,
            lax.dynamic_slice_in_dim(grad_key_acc, tile_start, window_span, 0) + grad_key,
            tile_start,
            0,
        )
        grad_value_acc = lax.dynamic_update_slice_in_dim(
            grad_value_acc,
            lax.dynamic_slice_in_dim(grad_value_acc, tile_start, window_span, 0) + grad_value,
            tile_start,
            0,
        )
        return ((grad_key_acc, grad_value_acc), (result, grad_query, stats))

    def cross_step(carry, tile_index):
        grad_key_acc, grad_value_acc = carry
        tile_start = tile_index * tile_rows
        query_tile = lax.dynamic_slice_in_dim(cross_query, tile_start, tile_rows, 0)
        grad_tile = lax.dynamic_slice_in_dim(cotangent, tile_start, tile_rows, 0)
        result, grad_query, grad_key, grad_value, stats = attend(
            query_tile, grad_tile, band[0], band[1], band_valid[None, :], heads_here
        )
        return ((grad_key_acc + grad_key, grad_value_acc + grad_value), (result, grad_query))

    zeros_ext = jnp.zeros((block_len + 2 * half_width, columns), jnp.float32)
    zeros_band = jnp.zeros((block_len, columns), jnp.float32)
    tile_ids = jnp.arange(tile_count)
    (self_gk, self_gv), (self_out, self_gq, self_stats) = lax.scan(
        self_step, (zeros_ext, zeros_ext), tile_ids
    )
    (cross_gk, cross_gv), (cross_out, cross_gq) = lax.scan(
        cross_step, (zeros_band, zeros_band), tile_ids
    )
    self_out = self_out.reshape(block_len, columns)
    cross_out = cross_out.reshape(block_len, columns)
    self_stats = jnp.transpose(self_stats, (1, 2, 0, 3)).reshape(3, heads_here, block_len)
    attended = (self_out + cross_out).astype(jnp.bfloat16)
    cross_ext = jnp.zeros((2, block_len + 2 * half_width, columns), jnp.float32)
    cross_ext = lax.dynamic_update_slice_in_dim(
        cross_ext, jnp.stack((cross_gk, cross_gv)), band_start, 1
    )
    self_ext = jnp.stack((self_gk, self_gv))
    self_core = self_ext[:, half_width : half_width + block_len]
    cross_core = cross_ext[:, half_width : half_width + block_len]
    upper_cut = block_len - half_width
    lower_send = jnp.concatenate((self_ext[:, :half_width], cross_ext[:, :half_width]), 0)
    upper_send = jnp.concatenate(
        (self_ext[:, block_len + half_width :], cross_ext[:, block_len + half_width :]), 0
    )
    from_above = passed_along(lower_send.astype(jnp.bfloat16), "blk", -1).astype(lower_send.dtype)
    from_below = passed_along(upper_send.astype(jnp.bfloat16), "blk", 1).astype(upper_send.dtype)
    self_core = (
        self_core.at[:, upper_cut:].add(from_above[:2]).at[:, :half_width].add(from_below[:2])
    )
    cross_core = (
        cross_core.at[:, upper_cut:].add(from_above[2:]).at[:, :half_width].add(from_below[2:])
    )
    returned = swapped(cross_core.astype(jnp.bfloat16), "tower", 0)
    head_outs = (
        attended,
        self_gq.reshape(block_len, columns).astype(jnp.bfloat16),
        self_core[0].astype(jnp.bfloat16),
        self_core[1].astype(jnp.bfloat16),
        cross_gq.reshape(block_len, columns).astype(jnp.bfloat16),
        returned[0],
        returned[1],
    )
    token_outs = (
        lax.all_to_all(head_outs[0], "seq", split_axis=0, concat_axis=1, tiled=True),
        lax.all_to_all(head_outs[1], "seq", split_axis=0, concat_axis=1, tiled=True),
        lax.all_to_all(head_outs[2], "seq", split_axis=0, concat_axis=1, tiled=True),
        lax.all_to_all(head_outs[3], "seq", split_axis=0, concat_axis=1, tiled=True),
        lax.all_to_all(head_outs[4], "seq", split_axis=0, concat_axis=1, tiled=True),
        lax.all_to_all(head_outs[5], "seq", split_axis=0, concat_axis=1, tiled=True),
        lax.all_to_all(head_outs[6], "seq", split_axis=0, concat_axis=1, tiled=True),
    )
    return tuple((piece[None] for piece in token_outs))


def solution(mesh):
    in_specs = (
        P("tower", ("blk", "seq"), None),
        P("tower", ("blk", "seq"), None),
        P("tower", ("blk", "seq"), None),
        P("tower", ("blk", "seq"), None),
        P("tower", ("blk", "seq"), None),
        P("tower", ("blk", "seq"), None),
        P("tower", ("blk", "seq"), None),
        P(),
        P(None, ("blk", "seq")),
    )
    out_specs = (
        P("tower", ("blk", "seq"), None),
        P("tower", ("blk", "seq"), None),
        P("tower", ("blk", "seq"), None),
        P("tower", ("blk", "seq"), None),
        P("tower", ("blk", "seq"), None),
        P("tower", ("blk", "seq"), None),
        P("tower", ("blk", "seq"), None),
    )
    body = paired if mesh.shape["seq"] == 2 else shards
    return jax.shard_map(body, mesh=mesh, in_specs=in_specs, out_specs=out_specs, check_vma=False)
```

```python
import functools

import jax
import jax.numpy as jnp
from jax import lax
from jax.experimental import pallas as pl
from jax.experimental.pallas import tpu as pltpu
from jax.sharding import PartitionSpec as P

HEADS = 16
HEAD = 64
WINDOW = 2048
TILE = 512
MESH = pl.DeviceIdType.MESH
F32, BF16 = jnp.float32, jnp.bfloat16


def places():
    tower, blk, seq = lax.axis_index("tower"), lax.axis_index("blk"), lax.axis_index("seq")
    peers = dict(
        y=(tower, blk, 1 - seq),
        tower=(1 - tower, blk, seq),
        diag=(1 - tower, blk, 1 - seq),
        low=(tower, blk - 1, seq),
        high=(tower, blk + 1, seq),
    )
    return tower, blk, seq, peers


def greet(blk, blks, peers):
    barrier = pltpu.get_barrier_semaphore()
    for name in ("y", "tower", "diag"):
        pl.semaphore_signal(barrier, inc=1, device_id=peers[name], device_id_type=MESH)

    @pl.when(blk > 0)
    def _():
        pl.semaphore_signal(barrier, inc=1, device_id=peers["low"], device_id_type=MESH)

    @pl.when(blk < blks - 1)
    def _():
        pl.semaphore_signal(barrier, inc=1, device_id=peers["high"], device_id_type=MESH)

    count = 3 + jnp.where(blk > 0, 1, 0) + jnp.where(blk < blks - 1, 1, 0)
    pl.semaphore_wait(barrier, count)


def remote(src, dst, send, recv, device):
    return pltpu.make_async_remote_copy(
        src_ref=src, dst_ref=dst, send_sem=send, recv_sem=recv,
        device_id=device, device_id_type=MESH,
    )


def fused_kernel(
    blks, rows, cols,
    off_ref, q_ref, k_ref, v_ref, cq_ref, ck_ref, cv_ref, g_ref, m_ref,
    o_out, gq_out, gk_out, gv_out, gcq_out, gck_out, gcv_out,
    side, ext, mask_ext, bias, y_stage, t_stage, low_stage, high_stage, core, recv,
    local_sem, mask_send, mask_recv, in_send, in_recv,
    low_send, low_recv, high_send, high_recv,
    out_send, out_recv, glow_send, glow_recv, ghigh_send, ghigh_recv,
):
    tower, blk, seq, peers = places()
    half, wide = rows, 2 * HEAD
    keys, groups = 3 * rows, cols // (2 * HEAD)
    scale = HEAD ** (-0.5)
    has_low, has_high = blk > 0, blk < blks - 1
    here = pl.ds(pl.multiple_of(seq * half, half), half)
    ext_here = pl.ds(pl.multiple_of((1 + seq) * half, half), half)
    mine = pl.ds(pl.multiple_of(seq * cols, cols), cols)
    inner_low, inner_high = pl.ds(half, half), pl.ds(2 * half, half)
    outer_low, outer_high = pl.ds(0, half), pl.ds(3 * half, half)
    direct = [o_out, gq_out, gcq_out]
    grads = [gk_out, gv_out, gck_out, gcv_out]

    def strip(g, base=0):
        return pl.ds(pl.multiple_of(base + g * wide, wide), wide)

    def incoming(g):
        at = strip(g)
        keep, give = strip(g, seq * cols), strip(g, (1 - seq) * cols)
        moves = [
            (k_ref.at[:, give], ext.at[0, ext_here, at], "y"),
            (v_ref.at[:, give], ext.at[1, ext_here, at], "y"),
            (ck_ref.at[:, give], ext.at[2, ext_here, at], "diag"),
            (cv_ref.at[:, give], ext.at[3, ext_here, at], "diag"),
            (ck_ref.at[:, keep], ext.at[2, ext_here, at], "tower"),
            (cv_ref.at[:, keep], ext.at[3, ext_here, at], "tower"),
            (q_ref.at[:, give], side.at[0, here, at], "y"),
            (g_ref.at[:, give], side.at[2, here, at], "y"),
            (cq_ref.at[:, give], side.at[1, here, at], "y"),
        ]
        return [
            remote(src, dst, in_send.at[g, i], in_recv.at[g, i], peers[to])
            for i, (src, dst, to) in enumerate(moves)
        ]

    def up(g, i):
        at = strip(g)
        return remote(
            ext.at[i, inner_high, at], ext.at[i, outer_low, at],
            high_send.at[g, i], high_recv.at[g, i], peers["high"],
        )

    def down(g, i):
        at = strip(g)
        return remote(
            ext.at[i, inner_low, at], ext.at[i, outer_high, at],
            low_send.at[g, i], low_recv.at[g, i], peers["low"],
        )

    mask_y = remote(m_ref, mask_ext.at[1 + seq], mask_send.at[0], mask_recv.at[0], peers["y"])
    mask_up = remote(mask_ext.at[2], mask_ext.at[0], mask_send.at[1], mask_recv.at[1], peers["high"])
    mask_down = remote(mask_ext.at[1], mask_ext.at[3], mask_send.at[2], mask_recv.at[2], peers["low"])

    def pass_on(g, own):
        moved = incoming(g)
        to_high = (seq == 1) if own else (seq == 0)
        to_low = (seq == 0) if own else (seq == 1)
        for i in range(4):
            if not own:
                moved[i].wait_recv()
            elif i >= 2:
                moved[i + 2].wait_recv()

            @pl.when(to_high & has_high)
            def _():
                up(g, i).start()

            @pl.when(to_low & has_low)
            def _():
                down(g, i).start()

    locals_ = [
        pltpu.make_async_copy(k_ref.at[:, mine], ext.at[0, ext_here, :], local_sem.at[0]),
        pltpu.make_async_copy(v_ref.at[:, mine], ext.at[1, ext_here, :], local_sem.at[1]),
        pltpu.make_async_copy(m_ref, mask_ext.at[1 + seq], local_sem.at[2]),
        pltpu.make_async_copy(q_ref.at[:, mine], side.at[0, here, :], local_sem.at[3]),
        pltpu.make_async_copy(cq_ref.at[:, mine], side.at[1, here, :], local_sem.at[4]),
        pltpu.make_async_copy(g_ref.at[:, mine], side.at[2, here, :], local_sem.at[5]),
    ]
    for copy in locals_:
        copy.start()

    @pl.when(blk == 0)
    def _():
        ext[:, :half, :] = jnp.zeros((4, half, cols), BF16)
        mask_ext[0] = jnp.zeros(mask_ext.shape[1:], jnp.int32)
        recv[0] = jnp.zeros(recv.shape[1:], BF16)

    @pl.when(blk == blks - 1)
    def _():
        ext[:, 3 * half :, :] = jnp.zeros((4, half, cols), BF16)
        mask_ext[3] = jnp.zeros(mask_ext.shape[1:], jnp.int32)
        recv[1] = jnp.zeros(recv.shape[1:], BF16)

    greet(blk, blks, peers)
    mask_y.start()
    for g in range(groups):
        for copy in incoming(g)[:6]:
            copy.start()
    for g in range(groups):
        for copy in incoming(g)[6:]:
            copy.start()
    for copy in locals_:
        copy.wait()
    pass_on(0, True)
    mask_y.wait_recv()

    @pl.when(has_high)
    def _():
        mask_up.start()

    @pl.when(has_low)
    def _():
        mask_down.start()

    for g in range(1, groups):
        pass_on(g, True)
    for g in range(groups):
        pass_on(g, False)

    @pl.when(has_high)
    def _():
        mask_down.wait_recv()

    @pl.when(has_low)
    def _():
        mask_up.wait_recv()

    off = off_ref[tower, blk]
    below = off < 0
    cross_at = jnp.where(below, 0, half)
    band_low = off + half

    def column(part, chain):
        row = jnp.where(
            chain == 0, mask_ext[part, 0:1, :].astype(F32), mask_ext[part, 1:2, :].astype(F32)
        )
        return jnp.transpose(jnp.broadcast_to(row, (half, half)))

    own_valid = [column(part, tower) for part in range(4)]
    other_valid = [column(part, 1 - tower) for part in range(4)]
    row_at = lax.broadcasted_iota(jnp.int32, (half, half), 0)
    col_at = lax.broadcasted_iota(jnp.int32, (half, half), 1)
    for part in range(3):
        where = slice(part * half, (part + 1) * half)
        distance = col_at + half - (row_at + part * half)
        for tile in range(2):
            near = (jnp.abs(distance) <= half) & (own_valid[tile + part] > 0)
            add = jnp.where(near, 0.0, -1e30)
            bias[tile, where, :half] = add
            bias[tile, where, half:] = add
        at = row_at + part * half + cross_at
        valid = jnp.where(below, other_valid[part], other_valid[part + 1])
        inside = (at >= band_low) & (at < band_low + 2 * half) & (valid > 0)
        add = jnp.where(inside, 0.0, -1e30)
        bias[2, where, :half] = add
        bias[2, where, half:] = add

    lanes = lax.broadcasted_iota(jnp.int32, (half, wide), 1)
    zero = jnp.zeros((half, wide), BF16)
    zero_half = jnp.zeros((half, wide), F32)

    def split(tile):
        return jnp.concatenate(
            (jnp.where(lanes < HEAD, tile, zero), jnp.where(lanes < HEAD, zero, tile)), 0
        )

    def dot_t(a, b):
        return lax.dot_general(a, b, (((1,), (1,)), ((), ())), preferred_element_type=F32)

    def dot(a, b):
        return jnp.dot(a, b, preferred_element_type=F32)

    def own_heads(both):
        return jnp.concatenate((both[:HEAD, :half], both[HEAD:, half:]), 0)

    def turned(x):
        return jnp.transpose(x.astype(F32)).astype(BF16)

    def one(query, cot, key, value, key_t, value_t, add):
        scores = dot_t(key, query) + bias[add]
        unnormed = jnp.exp(scores - jnp.max(scores, axis=0, keepdims=True))
        weights = unnormed * (1.0 / jnp.sum(unnormed, axis=0, keepdims=True))
        prob = weights.astype(BF16)
        grad_probs = dot_t(value, cot)
        row_dot = jnp.sum(weights * grad_probs, axis=0, keepdims=True)
        grad_scores = (weights * (grad_probs - row_dot)).astype(BF16)
        result = own_heads(dot(value_t, prob))
        grad_query = own_heads(dot(key_t, grad_scores)) * scale
        return result, grad_query, dot(grad_scores, query), dot(prob, cot)

    def compute(g):
        at = strip(g)
        key, value = ext[0, :, at], ext[1, :, at]
        ckey = jnp.where(below, ext[2, :keys, at], ext[2, half:, at])
        cvalue = jnp.where(below, ext[3, :keys, at], ext[3, half:, at])
        key_t, value_t, ckey_t, cvalue_t = turned(key), turned(value), turned(ckey), turned(cvalue)
        grad_parts, head_parts = [], []
        for tile in range(2):
            span = slice(tile * half, tile * half + keys)
            part = slice(tile * half, (tile + 1) * half)
            cot = split(side[2, part, at])
            query = split(side[0, part, at] * BF16(scale))
            cross = split(side[1, part, at] * BF16(scale))
            so, sq, sk, sv = one(
                query, cot, key[span], value[span], key_t[:, span], value_t[:, span], tile
            )
            co, cq, ck, cv = one(cross, cot, ckey, cvalue, ckey_t, cvalue_t, 2)
            head_parts.append((so + co, sq, cq))
            grad_parts.append((sk, sv, ck, cv))
        for i in range(2):
            first, second = grad_parts[0][i], grad_parts[1][i]
            low_stage[i, :, at] = first[:half].astype(BF16)
            core[i, 0, :, at] = first[half : 2 * half] + second[:half]
            core[i, 1, :, at] = first[2 * half :] + second[half : 2 * half]
            high_stage[i, :, at] = second[2 * half :].astype(BF16)
        for i in range(2, 4):
            total = grad_parts[0][i] + grad_parts[1][i]
            a, b, c = total[:half], total[half : 2 * half], total[2 * half :]
            low_stage[i, :, at] = jnp.where(below, a, zero_half).astype(BF16)
            core[i, 0, :, at] = jnp.where(below, b, a)
            core[i, 1, :, at] = jnp.where(below, c, b)
            high_stage[i, :, at] = jnp.where(below, zero_half, c).astype(BF16)
        for i in range(3):
            lower = turned(head_parts[0][i])
            upper = turned(head_parts[1][i])
            direct[i][:, strip(g, seq * cols)] = jnp.where(seq == 0, lower, upper)
            y_stage[i, :, at] = jnp.where(seq == 0, upper, lower)

    def grad_down(g, i):
        at = strip(g)
        return remote(
            low_stage.at[i, :, at], recv.at[1, i, :, at],
            glow_send.at[g, i], glow_recv.at[g, i], peers["low"],
        )

    def grad_up(g, i):
        at = strip(g)
        return remote(
            high_stage.at[i, :, at], recv.at[0, i, :, at],
            ghigh_send.at[g, i], ghigh_recv.at[g, i], peers["high"],
        )

    def outgoing(g):
        at, to_at = strip(g), strip(g, seq * cols)
        moves = [(y_stage.at[i, :, at], direct[i].at[:, to_at], "y") for i in range(3)]
        moves += [
            (y_stage.at[3 + i, :, at], grads[i].at[:, to_at], "y" if i < 2 else "diag")
            for i in range(4)
        ]
        moves += [(t_stage.at[i, :, at], grads[2 + i].at[:, to_at], "tower") for i in range(2)]
        return [
            remote(src, dst, out_send.at[g, i], out_recv.at[g, i], peers[to])
            for i, (src, dst, to) in enumerate(moves)
        ]

    def start_down(g):
        @pl.when(has_low)
        def _():
            for i in range(4):
                grad_down(g, i).start()

    def start_up(g):
        @pl.when(has_high)
        def _():
            for i in range(4):
                grad_up(g, i).start()

    def give(g):
        @pl.when(seq == 0)
        def _():
            start_down(g)
            start_up(g)

        @pl.when(seq == 1)
        def _():
            start_up(g)
            start_down(g)

        for copy in outgoing(g)[:3]:
            copy.start()

    def finish(g):
        at = strip(g)
        moves = outgoing(g)

        def take(low_side, high_side, i):
            @pl.when(low_side & has_low)
            def _():
                grad_up(g, i).wait_recv()

            @pl.when(high_side & has_high)
            def _():
                grad_down(g, i).wait_recv()

        for i in range(4):
            take(seq == 1, seq == 0, i)
            y_stage[3 + i, :, at] = (
                core[i, 1 - seq, :, at] + recv[1 - seq, i, :, at].astype(F32)
            ).astype(BF16)
            moves[3 + i].start()
        for i in (2, 3, 0, 1):
            take(seq == 0, seq == 1, i)
            total = (core[i, seq, :, at] + recv[seq, i, :, at].astype(F32)).astype(BF16)
            if i < 2:
                grads[i][:, strip(g, seq * cols)] = total
            else:
                t_stage[i - 2, :, at] = total
                moves[5 + i].start()

    def step(g, carry):
        for copy in incoming(g)[6:]:
            copy.wait_recv()

        @pl.when(has_high)
        def _():
            for i in range(4):
                down(g, i).wait_recv()

        @pl.when(has_low)
        def _():
            for i in range(4):
                up(g, i).wait_recv()

        compute(g)
        give(g)

        return carry

    lax.fori_loop(0, groups, step, 0)
    for g in range(groups):
        finish(g)

    def close(g, carry):
        for copy in incoming(g):
            copy.wait_send()
        for copy in outgoing(g):
            copy.wait()

        @pl.when(has_high)
        def _():
            for i in range(4):
                up(g, i).wait_send()
                grad_up(g, i).wait_send()

        @pl.when(has_low)
        def _():
            for i in range(4):
                down(g, i).wait_send()
                grad_down(g, i).wait_send()

        return carry

    lax.fori_loop(0, groups, close, 0)
    mask_y.wait_send()

    @pl.when(has_high)
    def _():
        mask_up.wait_send()

    @pl.when(has_low)
    def _():
        mask_down.wait_send()


def copy_kernel(*refs):
    count = len(refs) // 2
    for src, dst in zip(refs[:count], refs[count:]):
        dst[...] = src[...]


def paired(
    queries, key_rows, value_rows, cross_queries, cross_keys, cross_values, grad_out,
    offsets, key_valid,
):
    blks = lax.axis_size("blk")
    cols = HEADS // lax.axis_size("seq") * HEAD
    values = [
        value[0] for value in (
            queries, key_rows, value_rows, cross_queries, cross_keys, cross_values, grad_out
        )
    ]
    rows = queries.shape[1]
    block, groups = 2 * rows, cols // (2 * HEAD)
    vmem = pl.BlockSpec(memory_space=pltpu.VMEM)
    dma = pltpu.SemaphoreType.DMA
    full = jax.ShapeDtypeStruct((rows, 2 * cols), BF16)
    outs = pl.pallas_call(
        functools.partial(fused_kernel, blks, rows, cols),
        out_shape=(full,) * 7,
        in_specs=[pl.BlockSpec(memory_space=pltpu.SMEM)] + [pl.BlockSpec(memory_space=pl.ANY)] * 8,
        out_specs=(vmem,) * 7,
        scratch_shapes=[
            pltpu.VMEM((3, block, cols), BF16),
            pltpu.VMEM((4, 2 * block, cols), BF16),
            pltpu.VMEM((4,) + key_valid.shape, jnp.int32),
            pltpu.VMEM((3, 3 * rows, block), F32),
            pltpu.VMEM((7, rows, cols), BF16),
            pltpu.VMEM((2, rows, cols), BF16),
            pltpu.VMEM((4, rows, cols), BF16),
            pltpu.VMEM((4, rows, cols), BF16),
            pltpu.VMEM((4, 2, rows, cols), F32),
            pltpu.VMEM((2, 4, rows, cols), BF16),
            dma((6,)), dma((3,)), dma((3,)),
            dma((groups, 9)), dma((groups, 9)),
            dma((groups, 4)), dma((groups, 4)), dma((groups, 4)), dma((groups, 4)),
            dma((groups, 9)), dma((groups, 9)),
            dma((groups, 4)), dma((groups, 4)), dma((groups, 4)), dma((groups, 4)),
        ],
        compiler_params=pltpu.CompilerParams(collective_id=0, has_side_effects=True),
        name="attend_pairs",
    )(offsets, *values, key_valid)
    outs = pl.pallas_call(
        copy_kernel,
        out_shape=(full,) * 7,
        in_specs=[vmem] * 7,
        out_specs=(vmem,) * 7,
        name="hand_over",
    )(*outs)
    return tuple(piece[None] for piece in outs)


def extended(block, sides, width):
    for axis, dim in sides:
        count = lax.axis_size(axis)
        forward = [(i, i + 1) for i in range(count - 1)]
        backward = [(target, source) for source, target in forward]
        low = lax.ppermute(
            lax.slice_in_dim(block, block.shape[dim] - width, None, axis=dim), axis, forward
        )
        high = lax.ppermute(lax.slice_in_dim(block, 0, width, axis=dim), axis, backward)
        block = jnp.concatenate([low, block, high], axis=dim)
    return block


def swapped(value, axis, bit):
    mask = 2**bit
    pairs = [(source, source ^ mask) for source in range(lax.axis_size(axis))]
    return lax.ppermute(value, axis, pairs)


def passed_along(block, axis, distance):
    devices = range(lax.axis_size(axis))
    route = [(i - distance, i) for i in devices if i - distance in devices]
    return lax.ppermute(block, axis, route)


def attend(query_tile, grad_tile, key_block, value_block, allowed, heads_here):
    score_scale = HEAD ** (-0.5)
    rows_count = query_tile.shape[0]
    keys_count = key_block.shape[0]
    q_heads = query_tile.reshape(rows_count, heads_here, HEAD)
    g_heads = grad_tile.reshape(rows_count, heads_here, HEAD)
    k_heads = key_block.reshape(keys_count, heads_here, HEAD)
    v_heads = value_block.reshape(keys_count, heads_here, HEAD)
    scores = (
        jnp.einsum("qhe,khe->hqk", q_heads, k_heads, preferred_element_type=jnp.float32)
        * score_scale
    )
    scores = jnp.where(allowed[None], scores, -1e30)
    row_max = jnp.max(scores, axis=2)
    unnormed = jnp.exp(scores - row_max[:, :, None])
    row_sum = jnp.sum(unnormed, axis=2)
    weights = unnormed / row_sum[:, :, None]
    prob_bf = weights.astype(jnp.bfloat16)
    result = jnp.einsum(
        "hqk,khe->qhe", prob_bf, v_heads, preferred_element_type=jnp.float32
    ).reshape(rows_count, -1)
    grad_probs = jnp.einsum("qhe,khe->hqk", g_heads, v_heads, preferred_element_type=jnp.float32)
    row_dot = jnp.sum(weights * grad_probs, axis=2)
    grad_scores = (weights * (grad_probs - row_dot[:, :, None]) * score_scale).astype(jnp.bfloat16)
    grad_query = jnp.einsum(
        "hqk,khe->qhe", grad_scores, k_heads, preferred_element_type=jnp.float32
    ).reshape(rows_count, -1)
    grad_key = jnp.einsum(
        "hqk,qhe->khe", grad_scores, q_heads, preferred_element_type=jnp.float32
    ).reshape(keys_count, -1)
    grad_value = jnp.einsum(
        "hqk,qhe->khe", prob_bf, g_heads, preferred_element_type=jnp.float32
    ).reshape(keys_count, -1)
    return (result, grad_query, grad_key, grad_value, jnp.stack((row_max, row_sum, row_dot)))


def shards(
    queries,
    key_rows,
    value_rows,
    cross_queries,
    cross_keys,
    cross_values,
    grad_out,
    offsets,
    key_valid,
):
    seq_count = lax.axis_size("seq")
    heads_here = HEADS // seq_count
    local_rows = (
        queries[0],
        key_rows[0],
        value_rows[0],
        cross_queries[0],
        cross_keys[0],
        cross_values[0],
        grad_out[0],
    )
    query_here, key_here, value_here, cross_query, cross_key, cross_value, cotangent = (
        lax.all_to_all(local_rows[0], "seq", split_axis=1, concat_axis=0, tiled=True),
        lax.all_to_all(local_rows[1], "seq", split_axis=1, concat_axis=0, tiled=True),
        lax.all_to_all(local_rows[2], "seq", split_axis=1, concat_axis=0, tiled=True),
        lax.all_to_all(local_rows[3], "seq", split_axis=1, concat_axis=0, tiled=True),
        lax.all_to_all(local_rows[4], "seq", split_axis=1, concat_axis=0, tiled=True),
        lax.all_to_all(local_rows[5], "seq", split_axis=1, concat_axis=0, tiled=True),
        lax.all_to_all(local_rows[6], "seq", split_axis=1, concat_axis=0, tiled=True),
    )
    block_len = query_here.shape[0]
    columns = query_here.shape[1]
    half_width = min(WINDOW // 2, block_len // 2)
    tile_rows = min(TILE, block_len)
    tile_count = block_len // tile_rows
    window_span = tile_rows + 2 * half_width
    tower_id = lax.axis_index("tower")
    block_id = lax.axis_index("blk")
    block_mask = lax.all_gather(key_valid, "seq", axis=1, tiled=True)
    mask_ext = extended(block_mask, (("blk", 1),), half_width)
    self_valid = lax.dynamic_index_in_dim(mask_ext, tower_id, 0, keepdims=False)
    other_valid = lax.dynamic_index_in_dim(mask_ext, 1 - tower_id, 0, keepdims=False)
    pair_ext = extended(jnp.stack((key_here, value_here)), (("blk", 1),), half_width)
    partner = swapped(jnp.stack((cross_key, cross_value)), "tower", 0)
    partner_ext = extended(partner, (("blk", 1),), half_width)
    align_shift = offsets[tower_id, block_id]
    band_start = half_width + align_shift
    band = lax.dynamic_slice_in_dim(partner_ext, band_start, block_len, 1)
    band_valid = lax.dynamic_slice_in_dim(other_valid, band_start, block_len) > 0
    rows_local = jnp.arange(tile_rows)
    keys_local = jnp.arange(window_span)
    near = jnp.abs(rows_local[:, None] + half_width - keys_local[None, :]) <= half_width

    def self_step(carry, tile_index):
        grad_key_acc, grad_value_acc = carry
        tile_start = tile_index * tile_rows
        query_tile = lax.dynamic_slice_in_dim(query_here, tile_start, tile_rows, 0)
        grad_tile = lax.dynamic_slice_in_dim(cotangent, tile_start, tile_rows, 0)
        key_window = lax.dynamic_slice_in_dim(pair_ext[0], tile_start, window_span, 0)
        value_window = lax.dynamic_slice_in_dim(pair_ext[1], tile_start, window_span, 0)
        allowed = (
            near & (lax.dynamic_slice_in_dim(self_valid, tile_start, window_span) > 0)[None, :]
        )
        result, grad_query, grad_key, grad_value, stats = attend(
            query_tile, grad_tile, key_window, value_window, allowed, heads_here
        )
        grad_key_acc = lax.dynamic_update_slice_in_dim(
            grad_key_acc,
            lax.dynamic_slice_in_dim(grad_key_acc, tile_start, window_span, 0) + grad_key,
            tile_start,
            0,
        )
        grad_value_acc = lax.dynamic_update_slice_in_dim(
            grad_value_acc,
            lax.dynamic_slice_in_dim(grad_value_acc, tile_start, window_span, 0) + grad_value,
            tile_start,
            0,
        )
        return ((grad_key_acc, grad_value_acc), (result, grad_query, stats))

    def cross_step(carry, tile_index):
        grad_key_acc, grad_value_acc = carry
        tile_start = tile_index * tile_rows
        query_tile = lax.dynamic_slice_in_dim(cross_query, tile_start, tile_rows, 0)
        grad_tile = lax.dynamic_slice_in_dim(cotangent, tile_start, tile_rows, 0)
        result, grad_query, grad_key, grad_value, stats = attend(
            query_tile, grad_tile, band[0], band[1], band_valid[None, :], heads_here
        )
        return ((grad_key_acc + grad_key, grad_value_acc + grad_value), (result, grad_query))

    zeros_ext = jnp.zeros((block_len + 2 * half_width, columns), jnp.float32)
    zeros_band = jnp.zeros((block_len, columns), jnp.float32)
    tile_ids = jnp.arange(tile_count)
    (self_gk, self_gv), (self_out, self_gq, self_stats) = lax.scan(
        self_step, (zeros_ext, zeros_ext), tile_ids
    )
    (cross_gk, cross_gv), (cross_out, cross_gq) = lax.scan(
        cross_step, (zeros_band, zeros_band), tile_ids
    )
    self_out = self_out.reshape(block_len, columns)
    cross_out = cross_out.reshape(block_len, columns)
    self_stats = jnp.transpose(self_stats, (1, 2, 0, 3)).reshape(3, heads_here, block_len)
    attended = (self_out + cross_out).astype(jnp.bfloat16)
    cross_ext = jnp.zeros((2, block_len + 2 * half_width, columns), jnp.float32)
    cross_ext = lax.dynamic_update_slice_in_dim(
        cross_ext, jnp.stack((cross_gk, cross_gv)), band_start, 1
    )
    self_ext = jnp.stack((self_gk, self_gv))
    self_core = self_ext[:, half_width : half_width + block_len]
    cross_core = cross_ext[:, half_width : half_width + block_len]
    upper_cut = block_len - half_width
    lower_send = jnp.concatenate((self_ext[:, :half_width], cross_ext[:, :half_width]), 0)
    upper_send = jnp.concatenate(
        (self_ext[:, block_len + half_width :], cross_ext[:, block_len + half_width :]), 0
    )
    from_above = passed_along(lower_send.astype(jnp.bfloat16), "blk", -1).astype(lower_send.dtype)
    from_below = passed_along(upper_send.astype(jnp.bfloat16), "blk", 1).astype(upper_send.dtype)
    self_core = (
        self_core.at[:, upper_cut:].add(from_above[:2]).at[:, :half_width].add(from_below[:2])
    )
    cross_core = (
        cross_core.at[:, upper_cut:].add(from_above[2:]).at[:, :half_width].add(from_below[2:])
    )
    returned = swapped(cross_core.astype(jnp.bfloat16), "tower", 0)
    head_outs = (
        attended,
        self_gq.reshape(block_len, columns).astype(jnp.bfloat16),
        self_core[0].astype(jnp.bfloat16),
        self_core[1].astype(jnp.bfloat16),
        cross_gq.reshape(block_len, columns).astype(jnp.bfloat16),
        returned[0],
        returned[1],
    )
    token_outs = (
        lax.all_to_all(head_outs[0], "seq", split_axis=0, concat_axis=1, tiled=True),
        lax.all_to_all(head_outs[1], "seq", split_axis=0, concat_axis=1, tiled=True),
        lax.all_to_all(head_outs[2], "seq", split_axis=0, concat_axis=1, tiled=True),
        lax.all_to_all(head_outs[3], "seq", split_axis=0, concat_axis=1, tiled=True),
        lax.all_to_all(head_outs[4], "seq", split_axis=0, concat_axis=1, tiled=True),
        lax.all_to_all(head_outs[5], "seq", split_axis=0, concat_axis=1, tiled=True),
        lax.all_to_all(head_outs[6], "seq", split_axis=0, concat_axis=1, tiled=True),
    )
    return tuple((piece[None] for piece in token_outs))


def solution(mesh):
    in_specs = (
        P("tower", ("blk", "seq"), None),
        P("tower", ("blk", "seq"), None),
        P("tower", ("blk", "seq"), None),
        P("tower", ("blk", "seq"), None),
        P("tower", ("blk", "seq"), None),
        P("tower", ("blk", "seq"), None),
        P("tower", ("blk", "seq"), None),
        P(),
        P(None, ("blk", "seq")),
    )
    out_specs = (
        P("tower", ("blk", "seq"), None),
        P("tower", ("blk", "seq"), None),
        P("tower", ("blk", "seq"), None),
        P("tower", ("blk", "seq"), None),
        P("tower", ("blk", "seq"), None),
        P("tower", ("blk", "seq"), None),
        P("tower", ("blk", "seq"), None),
    )
    body = paired if mesh.shape["seq"] == 2 else shards
    return jax.shard_map(body, mesh=mesh, in_specs=in_specs, out_specs=out_specs, check_vma=False)
```

```python
import functools

import jax
import jax.numpy as jnp
from jax import lax
from jax.experimental import pallas as pl
from jax.experimental.pallas import tpu as pltpu
from jax.sharding import PartitionSpec as P

HEADS = 16
HEAD = 64
WINDOW = 2048
TILE = 512
MESH = pl.DeviceIdType.MESH
F32, BF16 = jnp.float32, jnp.bfloat16


def places():
    tower, blk, seq = lax.axis_index("tower"), lax.axis_index("blk"), lax.axis_index("seq")
    peers = dict(
        y=(tower, blk, 1 - seq),
        tower=(1 - tower, blk, seq),
        diag=(1 - tower, blk, 1 - seq),
        low=(tower, blk - 1, seq),
        high=(tower, blk + 1, seq),
    )
    return tower, blk, seq, peers


def greet(blk, blks, peers):
    barrier = pltpu.get_barrier_semaphore()
    for name in ("y", "tower", "diag"):
        pl.semaphore_signal(barrier, inc=1, device_id=peers[name], device_id_type=MESH)

    @pl.when(blk > 0)
    def _():
        pl.semaphore_signal(barrier, inc=1, device_id=peers["low"], device_id_type=MESH)

    @pl.when(blk < blks - 1)
    def _():
        pl.semaphore_signal(barrier, inc=1, device_id=peers["high"], device_id_type=MESH)

    count = 3 + jnp.where(blk > 0, 1, 0) + jnp.where(blk < blks - 1, 1, 0)
    pl.semaphore_wait(barrier, count)


def remote(src, dst, send, recv, device):
    return pltpu.make_async_remote_copy(
        src_ref=src, dst_ref=dst, send_sem=send, recv_sem=recv,
        device_id=device, device_id_type=MESH,
    )


def fused_kernel(
    blks, rows, cols,
    off_ref, q_ref, k_ref, v_ref, cq_ref, ck_ref, cv_ref, g_ref, m_ref,
    o_out, gq_out, gk_out, gv_out, gcq_out, gck_out, gcv_out,
    side, ext, mask_ext, bias, y_stage, t_stage, low_stage, high_stage, core, recv,
    local_sem, mask_send, mask_recv, in_send, in_recv,
    low_send, low_recv, high_send, high_recv,
    out_send, out_recv, glow_send, glow_recv, ghigh_send, ghigh_recv,
):
    tower, blk, seq, peers = places()
    half, wide = rows, 2 * HEAD
    keys, groups = 3 * rows, cols // (2 * HEAD)
    scale = HEAD ** (-0.5)
    has_low, has_high = blk > 0, blk < blks - 1
    here = pl.ds(pl.multiple_of(seq * half, half), half)
    ext_here = pl.ds(pl.multiple_of((1 + seq) * half, half), half)
    mine = pl.ds(pl.multiple_of(seq * cols, cols), cols)
    inner_low, inner_high = pl.ds(half, half), pl.ds(2 * half, half)
    outer_low, outer_high = pl.ds(0, half), pl.ds(3 * half, half)
    direct = [o_out, gq_out, gcq_out]
    grads = [gk_out, gv_out, gck_out, gcv_out]

    def strip(g, base=0):
        return pl.ds(pl.multiple_of(base + g * wide, wide), wide)

    def incoming(g):
        at = strip(g)
        keep, give = strip(g, seq * cols), strip(g, (1 - seq) * cols)
        moves = [
            (k_ref.at[:, give], ext.at[0, ext_here, at], "y"),
            (v_ref.at[:, give], ext.at[1, ext_here, at], "y"),
            (ck_ref.at[:, give], ext.at[2, ext_here, at], "diag"),
            (cv_ref.at[:, give], ext.at[3, ext_here, at], "diag"),
            (ck_ref.at[:, keep], ext.at[2, ext_here, at], "tower"),
            (cv_ref.at[:, keep], ext.at[3, ext_here, at], "tower"),
            (q_ref.at[:, give], side.at[0, here, at], "y"),
            (g_ref.at[:, give], side.at[2, here, at], "y"),
            (cq_ref.at[:, give], side.at[1, here, at], "y"),
        ]
        return [
            remote(src, dst, in_send.at[g, i], in_recv.at[g, i], peers[to])
            for i, (src, dst, to) in enumerate(moves)
        ]

    def up(g, i):
        at = strip(g)
        return remote(
            ext.at[pl.ds(2 * i, 2), inner_high, at], ext.at[pl.ds(2 * i, 2), outer_low, at],
            high_send.at[g, i], high_recv.at[g, i], peers["high"],
        )

    def down(g, i):
        at = strip(g)
        return remote(
            ext.at[pl.ds(2 * i, 2), inner_low, at], ext.at[pl.ds(2 * i, 2), outer_high, at],
            low_send.at[g, i], low_recv.at[g, i], peers["low"],
        )

    mask_y = remote(m_ref, mask_ext.at[1 + seq], mask_send.at[0], mask_recv.at[0], peers["y"])
    mask_up = remote(mask_ext.at[2], mask_ext.at[0], mask_send.at[1], mask_recv.at[1], peers["high"])
    mask_down = remote(mask_ext.at[1], mask_ext.at[3], mask_send.at[2], mask_recv.at[2], peers["low"])

    def pass_on(g, own):
        moved = incoming(g)
        to_high = (seq == 1) if own else (seq == 0)
        to_low = (seq == 0) if own else (seq == 1)
        for i in range(2):
            if not own:
                moved[2 * i].wait_recv()
                moved[2 * i + 1].wait_recv()
            elif i == 1:
                moved[4].wait_recv()
                moved[5].wait_recv()

            @pl.when(to_high & has_high)
            def _():
                up(g, i).start()

            @pl.when(to_low & has_low)
            def _():
                down(g, i).start()

    locals_ = [
        pltpu.make_async_copy(k_ref.at[:, mine], ext.at[0, ext_here, :], local_sem.at[0]),
        pltpu.make_async_copy(v_ref.at[:, mine], ext.at[1, ext_here, :], local_sem.at[1]),
        pltpu.make_async_copy(m_ref, mask_ext.at[1 + seq], local_sem.at[2]),
        pltpu.make_async_copy(q_ref.at[:, mine], side.at[0, here, :], local_sem.at[3]),
        pltpu.make_async_copy(cq_ref.at[:, mine], side.at[1, here, :], local_sem.at[4]),
        pltpu.make_async_copy(g_ref.at[:, mine], side.at[2, here, :], local_sem.at[5]),
    ]
    for copy in locals_:
        copy.start()

    @pl.when(blk == 0)
    def _():
        ext[:, :half, :] = jnp.zeros((4, half, cols), BF16)
        mask_ext[0] = jnp.zeros(mask_ext.shape[1:], jnp.int32)
        recv[0] = jnp.zeros(recv.shape[1:], BF16)

    @pl.when(blk == blks - 1)
    def _():
        ext[:, 3 * half :, :] = jnp.zeros((4, half, cols), BF16)
        mask_ext[3] = jnp.zeros(mask_ext.shape[1:], jnp.int32)
        recv[1] = jnp.zeros(recv.shape[1:], BF16)

    greet(blk, blks, peers)
    mask_y.start()
    for g in range(groups):
        for copy in incoming(g)[:6]:
            copy.start()
    for g in range(groups):
        for copy in incoming(g)[6:]:
            copy.start()
    for copy in locals_:
        copy.wait()
    pass_on(0, True)
    mask_y.wait_recv()

    @pl.when(has_high)
    def _():
        mask_up.start()

    @pl.when(has_low)
    def _():
        mask_down.start()

    for g in range(1, groups):
        pass_on(g, True)
    for g in range(groups):
        pass_on(g, False)

    @pl.when(has_high)
    def _():
        mask_down.wait_recv()

    @pl.when(has_low)
    def _():
        mask_up.wait_recv()

    off = off_ref[tower, blk]
    below = off < 0
    cross_at = jnp.where(below, 0, half)
    band_low = off + half

    def column(part, chain):
        row = jnp.where(
            chain == 0, mask_ext[part, 0:1, :].astype(F32), mask_ext[part, 1:2, :].astype(F32)
        )
        return jnp.transpose(jnp.broadcast_to(row, (half, half)))

    own_valid = [column(part, tower) for part in range(4)]
    other_valid = [column(part, 1 - tower) for part in range(4)]
    row_at = lax.broadcasted_iota(jnp.int32, (half, half), 0)
    col_at = lax.broadcasted_iota(jnp.int32, (half, half), 1)
    for part in range(3):
        where = slice(part * half, (part + 1) * half)
        distance = col_at + half - (row_at + part * half)
        for tile in range(2):
            near = (jnp.abs(distance) <= half) & (own_valid[tile + part] > 0)
            add = jnp.where(near, 0.0, -1e30)
            bias[tile, where, :half] = add
            bias[tile, where, half:] = add
        at = row_at + part * half + cross_at
        valid = jnp.where(below, other_valid[part], other_valid[part + 1])
        inside = (at >= band_low) & (at < band_low + 2 * half) & (valid > 0)
        add = jnp.where(inside, 0.0, -1e30)
        bias[2, where, :half] = add
        bias[2, where, half:] = add

    lanes = lax.broadcasted_iota(jnp.int32, (half, wide), 1)
    zero = jnp.zeros((half, wide), BF16)
    zero_half = jnp.zeros((half, wide), F32)

    def split(tile):
        return jnp.concatenate(
            (jnp.where(lanes < HEAD, tile, zero), jnp.where(lanes < HEAD, zero, tile)), 0
        )

    def dot_t(a, b):
        return lax.dot_general(a, b, (((1,), (1,)), ((), ())), preferred_element_type=F32)

    def dot(a, b):
        return jnp.dot(a, b, preferred_element_type=F32)

    def own_heads(both):
        return jnp.concatenate((both[:HEAD, :half], both[HEAD:, half:]), 0)

    def turned(x):
        return jnp.transpose(x.astype(F32)).astype(BF16)

    def one(query, cot, key, value, key_t, value_t, add):
        scores = dot_t(key, query) + bias[add]
        unnormed = jnp.exp(scores - jnp.max(scores, axis=0, keepdims=True))
        weights = unnormed * (1.0 / jnp.sum(unnormed, axis=0, keepdims=True))
        prob = weights.astype(BF16)
        grad_probs = dot_t(value, cot)
        row_dot = jnp.sum(weights * grad_probs, axis=0, keepdims=True)
        grad_scores = (weights * (grad_probs - row_dot)).astype(BF16)
        result = own_heads(dot(value_t, prob))
        grad_query = own_heads(dot(key_t, grad_scores)) * scale
        return result, grad_query, dot(grad_scores, query), dot(prob, cot)

    def compute(g):
        at = strip(g)
        key, value = ext[0, :, at], ext[1, :, at]
        ckey = jnp.where(below, ext[2, :keys, at], ext[2, half:, at])
        cvalue = jnp.where(below, ext[3, :keys, at], ext[3, half:, at])
        key_t, value_t, ckey_t, cvalue_t = turned(key), turned(value), turned(ckey), turned(cvalue)
        grad_parts, head_parts = [], []
        for tile in range(2):
            span = slice(tile * half, tile * half + keys)
            part = slice(tile * half, (tile + 1) * half)
            cot = split(side[2, part, at])
            query = split(side[0, part, at] * BF16(scale))
            cross = split(side[1, part, at] * BF16(scale))
            so, sq, sk, sv = one(
                query, cot, key[span], value[span], key_t[:, span], value_t[:, span], tile
            )
            co, cq, ck, cv = one(cross, cot, ckey, cvalue, ckey_t, cvalue_t, 2)
            head_parts.append((so + co, sq, cq))
            grad_parts.append((sk, sv, ck, cv))
        for i in range(2):
            first, second = grad_parts[0][i], grad_parts[1][i]
            low_stage[i, :, at] = first[:half].astype(BF16)
            core[i, 0, :, at] = first[half : 2 * half] + second[:half]
            core[i, 1, :, at] = first[2 * half :] + second[half : 2 * half]
            high_stage[i, :, at] = second[2 * half :].astype(BF16)
        for i in range(2, 4):
            total = grad_parts[0][i] + grad_parts[1][i]
            a, b, c = total[:half], total[half : 2 * half], total[2 * half :]
            low_stage[i, :, at] = jnp.where(below, a, zero_half).astype(BF16)
            core[i, 0, :, at] = jnp.where(below, b, a)
            core[i, 1, :, at] = jnp.where(below, c, b)
            high_stage[i, :, at] = jnp.where(below, zero_half, c).astype(BF16)
        for i in range(3):
            lower = turned(head_parts[0][i])
            upper = turned(head_parts[1][i])
            direct[i][:, strip(g, seq * cols)] = jnp.where(seq == 0, lower, upper)
            y_stage[i, :, at] = jnp.where(seq == 0, upper, lower)

    def grad_down(g, i):
        at = strip(g)
        return remote(
            low_stage.at[i, :, at], recv.at[1, i, :, at],
            glow_send.at[g, i], glow_recv.at[g, i], peers["low"],
        )

    def grad_up(g, i):
        at = strip(g)
        return remote(
            high_stage.at[i, :, at], recv.at[0, i, :, at],
            ghigh_send.at[g, i], ghigh_recv.at[g, i], peers["high"],
        )

    def outgoing(g):
        at, to_at = strip(g), strip(g, seq * cols)
        moves = [(y_stage.at[i, :, at], direct[i].at[:, to_at], "y") for i in range(3)]
        moves += [
            (y_stage.at[3 + i, :, at], grads[i].at[:, to_at], "y" if i < 2 else "diag")
            for i in range(4)
        ]
        moves += [(t_stage.at[i, :, at], grads[2 + i].at[:, to_at], "tower") for i in range(2)]
        return [
            remote(src, dst, out_send.at[g, i], out_recv.at[g, i], peers[to])
            for i, (src, dst, to) in enumerate(moves)
        ]

    def start_down(g):
        @pl.when(has_low)
        def _():
            for i in range(4):
                grad_down(g, i).start()

    def start_up(g):
        @pl.when(has_high)
        def _():
            for i in range(4):
                grad_up(g, i).start()

    def give(g):
        @pl.when(seq == 0)
        def _():
            start_down(g)
            start_up(g)

        @pl.when(seq == 1)
        def _():
            start_up(g)
            start_down(g)

        for copy in outgoing(g)[:3]:
            copy.start()

    def finish(g):
        at = strip(g)
        moves = outgoing(g)

        def take(low_side, high_side, i):
            @pl.when(low_side & has_low)
            def _():
                grad_up(g, i).wait_recv()

            @pl.when(high_side & has_high)
            def _():
                grad_down(g, i).wait_recv()

        for i in range(4):
            take(seq == 1, seq == 0, i)
            y_stage[3 + i, :, at] = (
                core[i, 1 - seq, :, at] + recv[1 - seq, i, :, at].astype(F32)
            ).astype(BF16)
            moves[3 + i].start()
        for i in (2, 3, 0, 1):
            take(seq == 0, seq == 1, i)
            total = (core[i, seq, :, at] + recv[seq, i, :, at].astype(F32)).astype(BF16)
            if i < 2:
                grads[i][:, strip(g, seq * cols)] = total
            else:
                t_stage[i - 2, :, at] = total
                moves[5 + i].start()

    def step(g, carry):
        for copy in incoming(g)[6:]:
            copy.wait_recv()

        @pl.when(has_high)
        def _():
            for i in range(2):
                down(g, i).wait_recv()

        @pl.when(has_low)
        def _():
            for i in range(2):
                up(g, i).wait_recv()

        compute(g)
        give(g)

        return carry

    lax.fori_loop(0, groups, step, 0)
    for g in range(groups):
        finish(g)

    def close(g, carry):
        for copy in incoming(g):
            copy.wait_send()
        for copy in outgoing(g):
            copy.wait()

        @pl.when(has_high)
        def _():
            for i in range(2):
                up(g, i).wait_send()
            for i in range(4):
                grad_up(g, i).wait_send()

        @pl.when(has_low)
        def _():
            for i in range(2):
                down(g, i).wait_send()
            for i in range(4):
                grad_down(g, i).wait_send()

        return carry

    lax.fori_loop(0, groups, close, 0)
    mask_y.wait_send()

    @pl.when(has_high)
    def _():
        mask_up.wait_send()

    @pl.when(has_low)
    def _():
        mask_down.wait_send()


def copy_kernel(*refs):
    count = len(refs) // 2
    for src, dst in zip(refs[:count], refs[count:]):
        dst[...] = src[...]


def paired(
    queries, key_rows, value_rows, cross_queries, cross_keys, cross_values, grad_out,
    offsets, key_valid,
):
    blks = lax.axis_size("blk")
    cols = HEADS // lax.axis_size("seq") * HEAD
    values = [
        value[0] for value in (
            queries, key_rows, value_rows, cross_queries, cross_keys, cross_values, grad_out
        )
    ]
    rows = queries.shape[1]
    block, groups = 2 * rows, cols // (2 * HEAD)
    vmem = pl.BlockSpec(memory_space=pltpu.VMEM)
    dma = pltpu.SemaphoreType.DMA
    full = jax.ShapeDtypeStruct((rows, 2 * cols), BF16)
    outs = pl.pallas_call(
        functools.partial(fused_kernel, blks, rows, cols),
        out_shape=(full,) * 7,
        in_specs=[pl.BlockSpec(memory_space=pltpu.SMEM)] + [pl.BlockSpec(memory_space=pl.ANY)] * 8,
        out_specs=(vmem,) * 7,
        scratch_shapes=[
            pltpu.VMEM((3, block, cols), BF16),
            pltpu.VMEM((4, 2 * block, cols), BF16),
            pltpu.VMEM((4,) + key_valid.shape, jnp.int32),
            pltpu.VMEM((3, 3 * rows, block), F32),
            pltpu.VMEM((7, rows, cols), BF16),
            pltpu.VMEM((2, rows, cols), BF16),
            pltpu.VMEM((4, rows, cols), BF16),
            pltpu.VMEM((4, rows, cols), BF16),
            pltpu.VMEM((4, 2, rows, cols), F32),
            pltpu.VMEM((2, 4, rows, cols), BF16),
            dma((6,)), dma((3,)), dma((3,)),
            dma((groups, 9)), dma((groups, 9)),
            dma((groups, 4)), dma((groups, 4)), dma((groups, 4)), dma((groups, 4)),
            dma((groups, 9)), dma((groups, 9)),
            dma((groups, 4)), dma((groups, 4)), dma((groups, 4)), dma((groups, 4)),
        ],
        compiler_params=pltpu.CompilerParams(collective_id=0, has_side_effects=True),
        name="attend_pairs",
    )(offsets, *values, key_valid)
    outs = pl.pallas_call(
        copy_kernel,
        out_shape=(full,) * 7,
        in_specs=[vmem] * 7,
        out_specs=(vmem,) * 7,
        name="hand_over",
    )(*outs)
    return tuple(piece[None] for piece in outs)


def extended(block, sides, width):
    for axis, dim in sides:
        count = lax.axis_size(axis)
        forward = [(i, i + 1) for i in range(count - 1)]
        backward = [(target, source) for source, target in forward]
        low = lax.ppermute(
            lax.slice_in_dim(block, block.shape[dim] - width, None, axis=dim), axis, forward
        )
        high = lax.ppermute(lax.slice_in_dim(block, 0, width, axis=dim), axis, backward)
        block = jnp.concatenate([low, block, high], axis=dim)
    return block


def swapped(value, axis, bit):
    mask = 2**bit
    pairs = [(source, source ^ mask) for source in range(lax.axis_size(axis))]
    return lax.ppermute(value, axis, pairs)


def passed_along(block, axis, distance):
    devices = range(lax.axis_size(axis))
    route = [(i - distance, i) for i in devices if i - distance in devices]
    return lax.ppermute(block, axis, route)


def attend(query_tile, grad_tile, key_block, value_block, allowed, heads_here):
    score_scale = HEAD ** (-0.5)
    rows_count = query_tile.shape[0]
    keys_count = key_block.shape[0]
    q_heads = query_tile.reshape(rows_count, heads_here, HEAD)
    g_heads = grad_tile.reshape(rows_count, heads_here, HEAD)
    k_heads = key_block.reshape(keys_count, heads_here, HEAD)
    v_heads = value_block.reshape(keys_count, heads_here, HEAD)
    scores = (
        jnp.einsum("qhe,khe->hqk", q_heads, k_heads, preferred_element_type=jnp.float32)
        * score_scale
    )
    scores = jnp.where(allowed[None], scores, -1e30)
    row_max = jnp.max(scores, axis=2)
    unnormed = jnp.exp(scores - row_max[:, :, None])
    row_sum = jnp.sum(unnormed, axis=2)
    weights = unnormed / row_sum[:, :, None]
    prob_bf = weights.astype(jnp.bfloat16)
    result = jnp.einsum(
        "hqk,khe->qhe", prob_bf, v_heads, preferred_element_type=jnp.float32
    ).reshape(rows_count, -1)
    grad_probs = jnp.einsum("qhe,khe->hqk", g_heads, v_heads, preferred_element_type=jnp.float32)
    row_dot = jnp.sum(weights * grad_probs, axis=2)
    grad_scores = (weights * (grad_probs - row_dot[:, :, None]) * score_scale).astype(jnp.bfloat16)
    grad_query = jnp.einsum(
        "hqk,khe->qhe", grad_scores, k_heads, preferred_element_type=jnp.float32
    ).reshape(rows_count, -1)
    grad_key = jnp.einsum(
        "hqk,qhe->khe", grad_scores, q_heads, preferred_element_type=jnp.float32
    ).reshape(keys_count, -1)
    grad_value = jnp.einsum(
        "hqk,qhe->khe", prob_bf, g_heads, preferred_element_type=jnp.float32
    ).reshape(keys_count, -1)
    return (result, grad_query, grad_key, grad_value, jnp.stack((row_max, row_sum, row_dot)))


def shards(
    queries,
    key_rows,
    value_rows,
    cross_queries,
    cross_keys,
    cross_values,
    grad_out,
    offsets,
    key_valid,
):
    seq_count = lax.axis_size("seq")
    heads_here = HEADS // seq_count
    local_rows = (
        queries[0],
        key_rows[0],
        value_rows[0],
        cross_queries[0],
        cross_keys[0],
        cross_values[0],
        grad_out[0],
    )
    query_here, key_here, value_here, cross_query, cross_key, cross_value, cotangent = (
        lax.all_to_all(local_rows[0], "seq", split_axis=1, concat_axis=0, tiled=True),
        lax.all_to_all(local_rows[1], "seq", split_axis=1, concat_axis=0, tiled=True),
        lax.all_to_all(local_rows[2], "seq", split_axis=1, concat_axis=0, tiled=True),
        lax.all_to_all(local_rows[3], "seq", split_axis=1, concat_axis=0, tiled=True),
        lax.all_to_all(local_rows[4], "seq", split_axis=1, concat_axis=0, tiled=True),
        lax.all_to_all(local_rows[5], "seq", split_axis=1, concat_axis=0, tiled=True),
        lax.all_to_all(local_rows[6], "seq", split_axis=1, concat_axis=0, tiled=True),
    )
    block_len = query_here.shape[0]
    columns = query_here.shape[1]
    half_width = min(WINDOW // 2, block_len // 2)
    tile_rows = min(TILE, block_len)
    tile_count = block_len // tile_rows
    window_span = tile_rows + 2 * half_width
    tower_id = lax.axis_index("tower")
    block_id = lax.axis_index("blk")
    block_mask = lax.all_gather(key_valid, "seq", axis=1, tiled=True)
    mask_ext = extended(block_mask, (("blk", 1),), half_width)
    self_valid = lax.dynamic_index_in_dim(mask_ext, tower_id, 0, keepdims=False)
    other_valid = lax.dynamic_index_in_dim(mask_ext, 1 - tower_id, 0, keepdims=False)
    pair_ext = extended(jnp.stack((key_here, value_here)), (("blk", 1),), half_width)
    partner = swapped(jnp.stack((cross_key, cross_value)), "tower", 0)
    partner_ext = extended(partner, (("blk", 1),), half_width)
    align_shift = offsets[tower_id, block_id]
    band_start = half_width + align_shift
    band = lax.dynamic_slice_in_dim(partner_ext, band_start, block_len, 1)
    band_valid = lax.dynamic_slice_in_dim(other_valid, band_start, block_len) > 0
    rows_local = jnp.arange(tile_rows)
    keys_local = jnp.arange(window_span)
    near = jnp.abs(rows_local[:, None] + half_width - keys_local[None, :]) <= half_width

    def self_step(carry, tile_index):
        grad_key_acc, grad_value_acc = carry
        tile_start = tile_index * tile_rows
        query_tile = lax.dynamic_slice_in_dim(query_here, tile_start, tile_rows, 0)
        grad_tile = lax.dynamic_slice_in_dim(cotangent, tile_start, tile_rows, 0)
        key_window = lax.dynamic_slice_in_dim(pair_ext[0], tile_start, window_span, 0)
        value_window = lax.dynamic_slice_in_dim(pair_ext[1], tile_start, window_span, 0)
        allowed = (
            near & (lax.dynamic_slice_in_dim(self_valid, tile_start, window_span) > 0)[None, :]
        )
        result, grad_query, grad_key, grad_value, stats = attend(
            query_tile, grad_tile, key_window, value_window, allowed, heads_here
        )
        grad_key_acc = lax.dynamic_update_slice_in_dim(
            grad_key_acc,
            lax.dynamic_slice_in_dim(grad_key_acc, tile_start, window_span, 0) + grad_key,
            tile_start,
            0,
        )
        grad_value_acc = lax.dynamic_update_slice_in_dim(
            grad_value_acc,
            lax.dynamic_slice_in_dim(grad_value_acc, tile_start, window_span, 0) + grad_value,
            tile_start,
            0,
        )
        return ((grad_key_acc, grad_value_acc), (result, grad_query, stats))

    def cross_step(carry, tile_index):
        grad_key_acc, grad_value_acc = carry
        tile_start = tile_index * tile_rows
        query_tile = lax.dynamic_slice_in_dim(cross_query, tile_start, tile_rows, 0)
        grad_tile = lax.dynamic_slice_in_dim(cotangent, tile_start, tile_rows, 0)
        result, grad_query, grad_key, grad_value, stats = attend(
            query_tile, grad_tile, band[0], band[1], band_valid[None, :], heads_here
        )
        return ((grad_key_acc + grad_key, grad_value_acc + grad_value), (result, grad_query))

    zeros_ext = jnp.zeros((block_len + 2 * half_width, columns), jnp.float32)
    zeros_band = jnp.zeros((block_len, columns), jnp.float32)
    tile_ids = jnp.arange(tile_count)
    (self_gk, self_gv), (self_out, self_gq, self_stats) = lax.scan(
        self_step, (zeros_ext, zeros_ext), tile_ids
    )
    (cross_gk, cross_gv), (cross_out, cross_gq) = lax.scan(
        cross_step, (zeros_band, zeros_band), tile_ids
    )
    self_out = self_out.reshape(block_len, columns)
    cross_out = cross_out.reshape(block_len, columns)
    self_stats = jnp.transpose(self_stats, (1, 2, 0, 3)).reshape(3, heads_here, block_len)
    attended = (self_out + cross_out).astype(jnp.bfloat16)
    cross_ext = jnp.zeros((2, block_len + 2 * half_width, columns), jnp.float32)
    cross_ext = lax.dynamic_update_slice_in_dim(
        cross_ext, jnp.stack((cross_gk, cross_gv)), band_start, 1
    )
    self_ext = jnp.stack((self_gk, self_gv))
    self_core = self_ext[:, half_width : half_width + block_len]
    cross_core = cross_ext[:, half_width : half_width + block_len]
    upper_cut = block_len - half_width
    lower_send = jnp.concatenate((self_ext[:, :half_width], cross_ext[:, :half_width]), 0)
    upper_send = jnp.concatenate(
        (self_ext[:, block_len + half_width :], cross_ext[:, block_len + half_width :]), 0
    )
    from_above = passed_along(lower_send.astype(jnp.bfloat16), "blk", -1).astype(lower_send.dtype)
    from_below = passed_along(upper_send.astype(jnp.bfloat16), "blk", 1).astype(upper_send.dtype)
    self_core = (
        self_core.at[:, upper_cut:].add(from_above[:2]).at[:, :half_width].add(from_below[:2])
    )
    cross_core = (
        cross_core.at[:, upper_cut:].add(from_above[2:]).at[:, :half_width].add(from_below[2:])
    )
    returned = swapped(cross_core.astype(jnp.bfloat16), "tower", 0)
    head_outs = (
        attended,
        self_gq.reshape(block_len, columns).astype(jnp.bfloat16),
        self_core[0].astype(jnp.bfloat16),
        self_core[1].astype(jnp.bfloat16),
        cross_gq.reshape(block_len, columns).astype(jnp.bfloat16),
        returned[0],
        returned[1],
    )
    token_outs = (
        lax.all_to_all(head_outs[0], "seq", split_axis=0, concat_axis=1, tiled=True),
        lax.all_to_all(head_outs[1], "seq", split_axis=0, concat_axis=1, tiled=True),
        lax.all_to_all(head_outs[2], "seq", split_axis=0, concat_axis=1, tiled=True),
        lax.all_to_all(head_outs[3], "seq", split_axis=0, concat_axis=1, tiled=True),
        lax.all_to_all(head_outs[4], "seq", split_axis=0, concat_axis=1, tiled=True),
        lax.all_to_all(head_outs[5], "seq", split_axis=0, concat_axis=1, tiled=True),
        lax.all_to_all(head_outs[6], "seq", split_axis=0, concat_axis=1, tiled=True),
    )
    return tuple((piece[None] for piece in token_outs))


def solution(mesh):
    in_specs = (
        P("tower", ("blk", "seq"), None),
        P("tower", ("blk", "seq"), None),
        P("tower", ("blk", "seq"), None),
        P("tower", ("blk", "seq"), None),
        P("tower", ("blk", "seq"), None),
        P("tower", ("blk", "seq"), None),
        P("tower", ("blk", "seq"), None),
        P(),
        P(None, ("blk", "seq")),
    )
    out_specs = (
        P("tower", ("blk", "seq"), None),
        P("tower", ("blk", "seq"), None),
        P("tower", ("blk", "seq"), None),
        P("tower", ("blk", "seq"), None),
        P("tower", ("blk", "seq"), None),
        P("tower", ("blk", "seq"), None),
        P("tower", ("blk", "seq"), None),
    )
    body = paired if mesh.shape["seq"] == 2 else shards
    return jax.shard_map(body, mesh=mesh, in_specs=in_specs, out_specs=out_specs, check_vma=False)
```
